256 devices in a mesh: dp: 4 (over x), expert: 32 (over z, y), tensor: 2 (over core).
Axes of the slice: x: 4, y: 4, z: 8, core: 2. Of those that a mesh axis runs over, the one named last changes fastest.
Arguments:
- queries: bfloat16 [8192, 4096], P(('dp', 'expert'), 'tensor'), may hold values from -8 to 8
- fresh_keys: bfloat16 [8192, 512], P(('dp', 'expert'), 'tensor'), may hold values from -6 to 6
- fresh_values: bfloat16 [8192, 512], P(('dp', 'expert'), 'tensor'), may hold values from -6 to 6
- resident_keys: bfloat16 [128, 2048, 512], P(('dp', 'expert'), None, 'tensor'), may hold values from -8 to 8
- resident_values: bfloat16 [128, 2048, 512], P(('dp', 'expert'), None, 'tensor'), may hold values from -6 to 6
- out_weight: bfloat16 [4096, 2048], P('tensor', 'dp'), may hold values from -0.5 to 0.5
- residual: bfloat16 [8192, 2048], P(('dp', 'expert')), may hold values from -23 to 23
- norm_gain: float32 [2048], replicated, may hold values from 0.1 to 1.9
- expert_ids: int32 [8192, 8], P(('dp', 'expert')), may hold values from 0 to 127, all different within a row; in each aligned block of 64 rows (0 to 63, 64 to 127, ...) at most 6 rows name the same one
- gates: float32 [8192, 8], P(('dp', 'expert')), may hold values from 0.05 to 0.5
- w_gate: bfloat16 [128, 2048, 768], P(('dp', 'expert'), None, 'tensor'), may hold values from -0.125 to 0.125
- w_up: bfloat16 [128, 2048, 768], P(('dp', 'expert'), None, 'tensor'), may hold values from -0.125 to 0.125
- w_down: bfloat16 [128, 768, 2048], P(('dp', 'expert'), 'tensor'), may hold values from -0.21875 to 0.21875
Outputs:
- mixed: bfloat16 [8192, 2048], P(('dp', 'expert'), 'tensor')
The draws below stay inside these ranges and needn't reach their ends.
Inputs may be any that keep to these rules, and one draw needn't show every extreme that they name: `expert_ids`: within the 64 tokens of one sequence no expert is named by more than 6 tokens, a bound that some block reaches; a token names 8 different experts.
All inputs are finite; a program needn't handle non-finite values.
Results may differ from the reference program's by a relative error of at most 0.0085.
Values may be sent and summed in bfloat16 or wider, within the bound.
No kernel may reach another device: no remote copies, remote signals or barrier semaphores. Data moves between devices by JAX's collectives and lax.ppermute only.
A program may use at most 64 MiB of HBM per device.

```python
import math
import jax
import jax.numpy as jnp
import numpy as np
from jax import lax

D = 2048
QUERY_HEADS = 32
KEY_VALUE_HEADS = 4
HEAD_WIDTH = 128
FFE = 768
TOP = 8
TOKENS_PER_SEQ = 64
CACHED_SPAN = 2048
EXPERTS = 128
SEQUENCE_COUNT = 128
TOKEN_COUNT = 8192
CAP = 6


def draw_queries(key, part):
    base_offset = jnp.clip(jax.random.normal(jax.random.fold_in(key, 1), (TOKEN_COUNT, QUERY_HEADS * HEAD_WIDTH), jnp.float32), -6.0, 6.0)
    return base_offset.astype(jnp.bfloat16)


def draw_resident_keys(key, part):
    base_offset = jnp.clip(jax.random.normal(jax.random.fold_in(key, 2), (SEQUENCE_COUNT, CACHED_SPAN, KEY_VALUE_HEADS * HEAD_WIDTH), jnp.float32), -6.0, 6.0)
    return base_offset.astype(jnp.bfloat16)


def draw_residual(key, part):
    column = jnp.arange(D, dtype=jnp.float32) / D
    column_scale = jnp.power(10.0, column - 0.5)
    row_draw = jax.random.uniform(jax.random.fold_in(key, 3), (TOKEN_COUNT, 1), jnp.float32)
    row_scale = jnp.power(10.0, 0.5 * row_draw - 0.25)
    base_offset = jnp.clip(jax.random.normal(jax.random.fold_in(key, 4), (TOKEN_COUNT, D), jnp.float32), -4.0, 4.0)
    return (base_offset * column_scale[None, :] * row_scale).astype(jnp.bfloat16)


def block_levels(key, dims, shards, smallest, top_value):
    level, own = 1.0, jax.random.fold_in(key, 6)
    for position, blocks in shards:
        steps = jnp.exp(jax.random.uniform(jax.random.fold_in(own, position), (blocks,), jnp.float32, smallest / len(shards), top_value / len(shards)))
        level = level * jnp.repeat(steps, dims[position] // blocks).reshape([-1 if axis == position else 1 for axis in range(len(dims))])
    return level


def routed_block(key, own, number, rows, number_of, top, limit, skew):
    order = jax.random.permutation(key, number_of)
    packed, usual = load_shares(number_of, rows * top, limit, skew, True), load_shares(number_of, rows * top, limit, skew, False)
    places = jnp.arange(number_of)

    def named(tallies, turn):
        used = int((tallies > 0).sum())
        fixed = max(1, used // 4)
        passed = fixed + (places - fixed + turn * (used - fixed)) % max(1, number_of - fixed)
        return jnp.zeros((number_of,), jnp.int32).at[order[jnp.where(places < fixed, places, passed)]].set(jnp.asarray(tallies, jnp.int32))

    tallies = jnp.where(number % 4 == 0, named(packed, number // 4), named(usual, number - number // 4 - 1))
    mixed = jax.random.permutation(jax.random.fold_in(own, 3), number_of)
    source_of, receiver = mixed[0:number_of // 2 * 2:2], mixed[1:number_of // 2 * 2:2]
    margin = jnp.minimum(tallies[source_of] - 1, limit - tallies[receiver]) // 2
    margin = jnp.where((source_of == order[0]) | (receiver == order[0]) | (tallies[receiver] == 0), 0, jnp.maximum(margin, 0))
    passed = jax.random.randint(jax.random.fold_in(own, 4), (number_of // 2,), 0, 1 << 20) % (margin + 1)
    tallies = tallies.at[source_of].add(-passed).at[receiver].add(passed)
    labels = jnp.searchsorted(jnp.cumsum(tallies), jnp.arange(rows * top), side="right").astype(jnp.int32)
    listing = labels.reshape(top, rows).T
    listing = listing[jax.random.permutation(jax.random.fold_in(own, 1), rows)]
    turn = jax.random.randint(jax.random.fold_in(own, 2), (rows, 1), 0, top)
    return jnp.take_along_axis(listing, (jnp.arange(top)[None, :] + turn) % top, axis=1)


def load_shares(count, total, bound, lean, full):
    weights = [(1 << 20) // math.isqrt(rank ** lean) + 1 for rank in range(1, count + 1)]
    largest = bound if full else min(bound, max(-(-total // count), total * weights[0] // sum(weights)))
    least = 1 if total - largest >= count - 1 else 0
    holding, rest = [largest] + [least] * (count - 1), total - largest - least * (count - 1)
    while rest > 0:
        free = [i for i in range(1, count) if holding[i] < largest] or [i for i in range(1, count) if holding[i] < bound]
        whole, left = sum([weights[i] for i in free]), rest
        for i in free:
            extra = min(bound - holding[i], max(1, left * weights[i] // whole), rest)
            holding[i] = holding[i] + extra
            rest = rest - extra
    return np.array(holding)


def scatter_about(key, shape, width, bound, shards=(), kind=jnp.bfloat16):
    level = block_levels(key, shape, shards, -0.22, 0.18) if shards else 1.0
    result = jax.random.normal(key, shape, jnp.float32) * width * level
    return jnp.minimum(jnp.maximum(result, -bound), bound).astype(kind)


def setup_inputs(seed: int = 0) -> dict:
    streams_of = jax.random.split(jax.random.key(seed), 14)
    queries = draw_queries(jax.random.fold_in(streams_of[13], 71), 0)
    fresh_keys = scatter_about(streams_of[1], (TOKEN_COUNT, KEY_VALUE_HEADS * HEAD_WIDTH), 1.0, 6.0, ((0, 128), (1, 2)))
    fresh_values = scatter_about(streams_of[2], (TOKEN_COUNT, KEY_VALUE_HEADS * HEAD_WIDTH), 1.0, 6.0, ((0, 128), (1, 2)))
    resident_keys = draw_resident_keys(jax.random.fold_in(streams_of[13], 71), 0)
    resident_values = scatter_about(streams_of[4], (SEQUENCE_COUNT, CACHED_SPAN, KEY_VALUE_HEADS * HEAD_WIDTH), 1.0, 6.0, ((0, 128), (2, 2)))
    out_weight = scatter_about(streams_of[5], (QUERY_HEADS * HEAD_WIDTH, D), HEAD_WIDTH ** -0.5, 0.5, ((0, 2), (1, 4)))
    residual = draw_residual(jax.random.fold_in(streams_of[13], 71), 0)
    norm_gain = jnp.clip(1.0 + 0.18 * jax.random.normal(streams_of[7], (D,), jnp.float32), 0.1, 1.9)
    expert_ids_keys = jax.random.split(jax.random.fold_in(streams_of[8], 1), TOKEN_COUNT // TOKENS_PER_SEQ)
    expert_ids_turns = jax.random.permutation(jax.random.fold_in(streams_of[8], 3), TOKEN_COUNT // TOKENS_PER_SEQ)
    expert_ids = jax.vmap(lambda own, number: routed_block(jax.random.fold_in(streams_of[8], 2), own, number, TOKENS_PER_SEQ, EXPERTS, TOP, CAP, 2))(expert_ids_keys, expert_ids_turns).reshape((TOKEN_COUNT, TOP))
    gates = jnp.clip(jnp.exp(math.log(0.5) - 2.3025851 * jax.random.uniform(streams_of[9], (TOKEN_COUNT, TOP), jnp.float32) ** block_levels(streams_of[9], (TOKEN_COUNT, TOP), ((0, 128),), -0.2, 0.2)), 0.05, 0.5)
    w_gate = scatter_about(streams_of[10], (EXPERTS, D, FFE), D ** -0.5, 0.125, ((0, 128), (2, 2)))
    w_up = scatter_about(streams_of[11], (EXPERTS, D, FFE), D ** -0.5, 0.125, ((0, 128), (2, 2)))
    w_down = scatter_about(streams_of[12], (EXPERTS, FFE, D), FFE ** -0.5, 0.21875, ((0, 128), (1, 2)))
    return {"queries": queries, "fresh_keys": fresh_keys, "fresh_values": fresh_values, "resident_keys": resident_keys, "resident_values": resident_values, "out_weight": out_weight, "residual": residual, "norm_gain": norm_gain, "expert_ids": expert_ids, "gates": gates, "w_gate": w_gate, "w_up": w_up, "w_down": w_down}


def attend_one(pack):
    query_rows, fresh_key, fresh_value, prior_key, prior_value = pack
    query_group = QUERY_HEADS // KEY_VALUE_HEADS
    query_rows = query_rows.astype(jnp.float32).reshape(TOKENS_PER_SEQ, KEY_VALUE_HEADS, query_group, HEAD_WIDTH)
    joined_keys = jnp.concatenate([prior_key, fresh_key], 0).astype(jnp.float32).reshape(CACHED_SPAN + TOKENS_PER_SEQ, KEY_VALUE_HEADS, HEAD_WIDTH)
    joined_values = jnp.concatenate([prior_value, fresh_value], 0).astype(jnp.float32).reshape(CACHED_SPAN + TOKENS_PER_SEQ, KEY_VALUE_HEADS, HEAD_WIDTH)
    score = jnp.einsum('tjgd,sjd->jgts', query_rows, joined_keys) * HEAD_WIDTH ** (-0.5)
    places = jnp.arange(CACHED_SPAN + TOKENS_PER_SEQ)
    rows = jnp.arange(TOKENS_PER_SEQ)
    allowed = (places[None, :] < CACHED_SPAN) | (places[None, :] - CACHED_SPAN <= rows[:, None])
    score = jnp.where(allowed, score, jnp.float32(-1e+30))
    top_score = lax.optimization_barrier(jnp.max(score, axis=-1, keepdims=True))
    weight = jnp.exp(score - top_score)
    probs = (weight / lax.optimization_barrier(jnp.sum(weight, axis=-1, keepdims=True))).astype(jnp.bfloat16)
    attended = jnp.einsum('jgts,sjd->tjgd', probs.astype(jnp.float32), joined_values)
    return attended.reshape(TOKENS_PER_SEQ, QUERY_HEADS * HEAD_WIDTH).astype(jnp.bfloat16)

def block_slots(block_ids):
    onehot = (block_ids[:, :, None] == jnp.arange(EXPERTS)[None, None, :]).astype(jnp.int32)
    per_token = lax.optimization_barrier(jnp.sum(onehot, axis=1))
    before = jnp.cumsum(per_token, axis=0) - per_token
    slot = lax.optimization_barrier(jnp.sum(onehot * before[:, None, :], axis=-1)).astype(jnp.int32)
    token_rows = jnp.broadcast_to(jnp.arange(TOKENS_PER_SEQ, dtype=jnp.int32)[:, None], block_ids.shape)
    owner_rows = jnp.full((EXPERTS, CAP), -1, jnp.int32).at[block_ids, slot].set(token_rows)
    return owner_rows

def reference(queries, fresh_keys, fresh_values, resident_keys, resident_values, out_weight, residual, norm_gain, expert_ids, gates, w_gate, w_up, w_down):
    packed_groups = (queries.reshape(SEQUENCE_COUNT, TOKENS_PER_SEQ, QUERY_HEADS * HEAD_WIDTH), fresh_keys.reshape(SEQUENCE_COUNT, TOKENS_PER_SEQ, KEY_VALUE_HEADS * HEAD_WIDTH), fresh_values.reshape(SEQUENCE_COUNT, TOKENS_PER_SEQ, KEY_VALUE_HEADS * HEAD_WIDTH), resident_keys, resident_values)
    attended = lax.map(attend_one, packed_groups).reshape(TOKEN_COUNT, QUERY_HEADS * HEAD_WIDTH)
    projected = jnp.dot(attended, out_weight, preferred_element_type=jnp.float32)
    hidden = residual.astype(jnp.float32) + projected
    mean_square = lax.optimization_barrier(jnp.mean(hidden * hidden, axis=-1, keepdims=True))
    normed = (hidden * lax.rsqrt(mean_square + 1e-06) * norm_gain).astype(jnp.bfloat16)
    owner_rows = jax.vmap(block_slots)(expert_ids.reshape(SEQUENCE_COUNT, TOKENS_PER_SEQ, TOP))
    offsets = (jnp.arange(SEQUENCE_COUNT, dtype=jnp.int32) * TOKENS_PER_SEQ)[:, None]

    def one_expert(total, pack):
        gate_mat, up_mat, down_mat, index = pack
        local = owner_rows[:, index, :]
        valid = (local >= 0).reshape(-1)
        spots = jnp.where(local >= 0, local + offsets, 0).reshape(-1).astype(jnp.int32)
        rows = jnp.where(valid[:, None], normed[spots], jnp.zeros((), jnp.bfloat16))
        gate_part = jnp.dot(rows, gate_mat, preferred_element_type=jnp.float32)
        up_part = jnp.dot(rows, up_mat, preferred_element_type=jnp.float32)
        act = (jax.nn.silu(gate_part) * up_part).astype(jnp.bfloat16)
        out = jnp.dot(act, down_mat, preferred_element_type=jnp.float32).astype(jnp.bfloat16)
        chosen = lax.optimization_barrier(jnp.sum(jnp.where(expert_ids == index, gates, jnp.float32(0.0)), axis=1))
        scale = jnp.where(valid, chosen[spots], jnp.float32(0.0))
        total = total.at[spots].add(scale[:, None] * out.astype(jnp.float32))
        return (total, None)
    start = jnp.zeros((TOKEN_COUNT, D), jnp.float32)
    moe, unused = lax.scan(one_expert, start, (w_gate, w_up, w_down, jnp.arange(EXPERTS, dtype=jnp.int32)))
    return (hidden + moe).astype(jnp.bfloat16)
```

```python
import jax
import jax.numpy as jnp
from jax import lax
from jax.sharding import PartitionSpec as P

D = 2048
HEAD_WIDTH = 128
CAP = 6


def attend_local(queries, fresh_keys, fresh_values, resident_keys, resident_values):
    tokens_here = queries.shape[0]
    kv_here = fresh_keys.shape[1] // HEAD_WIDTH
    query_group = queries.shape[1] // HEAD_WIDTH // kv_here
    context = resident_keys.shape[1]
    query_rows = queries.reshape(tokens_here, kv_here, query_group, HEAD_WIDTH)
    joined_keys = jnp.concatenate([resident_keys[0], fresh_keys], 0).reshape(
        context + tokens_here, kv_here, HEAD_WIDTH
    )
    joined_values = jnp.concatenate([resident_values[0], fresh_values], 0).reshape(
        context + tokens_here, kv_here, HEAD_WIDTH
    )
    score = jnp.einsum(
        "tjgd,sjd->jgts", query_rows, joined_keys, preferred_element_type=jnp.float32
    ) * HEAD_WIDTH ** (-0.5)
    places = jnp.arange(context + tokens_here)
    rows = jnp.arange(tokens_here)
    allowed = (places[None, :] < context) | (places[None, :] - context <= rows[:, None])
    score = jnp.where(allowed, score, jnp.float32(-1e30))
    top_score = jnp.max(score, axis=-1, keepdims=True)
    weight = jnp.exp(score - top_score)
    probs = (weight / jnp.sum(weight, axis=-1, keepdims=True)).astype(jnp.bfloat16)
    attended = jnp.einsum(
        "jgts,sjd->tjgd", probs, joined_values, preferred_element_type=jnp.float32
    )
    return attended.reshape(tokens_here, -1).astype(jnp.bfloat16)


def swap_pair(x):
    return lax.ppermute(x, "tensor", [(0, 1), (1, 0)])


def per_device(
    queries,
    fresh_keys,
    fresh_values,
    resident_keys,
    resident_values,
    out_weight,
    residual,
    norm_gain,
    expert_ids,
    gates,
    w_gate,
    w_up,
    w_down,
):
    tokens_here = residual.shape[0]
    lane = lax.axis_index("tensor")
    half = D // lax.axis_size("tensor")
    groups = lax.axis_size("dp")
    attended = attend_local(queries, fresh_keys, fresh_values, resident_keys, resident_values)

    gathered = lax.all_gather(attended, "dp", axis=0, tiled=True)
    part = jnp.dot(gathered, out_weight, preferred_element_type=jnp.float32)
    part = part.reshape(groups, tokens_here, -1)
    mine = lax.all_to_all(part, "dp", split_axis=0, concat_axis=0, tiled=True)
    mine = mine.transpose(1, 0, 2).reshape(tokens_here, D)
    summed = mine + swap_pair(mine)
    hidden = residual.astype(jnp.float32) + summed
    mean_square = jnp.mean(hidden * hidden, axis=-1, keepdims=True)
    normed = (hidden * lax.rsqrt(mean_square + 1e-06) * norm_gain).astype(jnp.bfloat16)
    hidden_half = lax.dynamic_slice_in_dim(hidden, lane * half, half, 1)
    normed_half = lax.dynamic_slice_in_dim(normed, lane * half, half, 1)

    owners = lax.axis_size("dp") * lax.axis_size("expert")
    onehot = (expert_ids[:, :, None] == jnp.arange(owners)[None, None, :]).astype(jnp.int32)
    per_token = jnp.sum(onehot, axis=1)
    before = jnp.cumsum(per_token, axis=0) - per_token
    slot = jnp.sum(onehot * before[:, None, :], axis=-1)
    code = expert_ids * CAP + slot
    pick = (code[:, :, None] == jnp.arange(owners * CAP)[None, None, :]).astype(jnp.bfloat16)
    spread = jnp.sum(pick, axis=1)
    outgoing = jnp.einsum(
        "tr,tf->rf", spread, normed_half, preferred_element_type=jnp.float32
    ).astype(jnp.bfloat16)
    received = lax.all_to_all(
        outgoing.reshape(owners, CAP, half), ("dp", "expert"), split_axis=0, concat_axis=0, tiled=True
    ).reshape(owners * CAP, half)
    other = swap_pair(received)
    first = jnp.where(lane == 0, received, other)
    second = jnp.where(lane == 0, other, received)
    flat = jnp.concatenate([first, second], axis=1)

    gate_part = jnp.dot(flat, w_gate[0], preferred_element_type=jnp.float32)
    up_part = jnp.dot(flat, w_up[0], preferred_element_type=jnp.float32)
    act = (jax.nn.silu(gate_part) * up_part).astype(jnp.bfloat16)
    result = jnp.dot(act, w_down[0], preferred_element_type=jnp.float32)
    own = lax.dynamic_slice_in_dim(result, lane * half, half, 1)
    theirs = lax.dynamic_slice_in_dim(result, (1 - lane) * half, half, 1)
    expert_out = (own + swap_pair(theirs)).astype(jnp.bfloat16)

    returned = lax.all_to_all(
        expert_out.reshape(owners, CAP, half), ("dp", "expert"), split_axis=0, concat_axis=0, tiled=True
    ).reshape(owners * CAP, half)
    picked = jnp.einsum("tkr,rf->tkf", pick, returned, preferred_element_type=jnp.float32)
    moe = jnp.sum(gates[:, :, None] * picked, axis=1)
    return (hidden_half + moe).astype(jnp.bfloat16)


def solution(mesh):
    return jax.shard_map(
        per_device,
        mesh=mesh,
        in_specs=(
            P(("dp", "expert"), "tensor"),
            P(("dp", "expert"), "tensor"),
            P(("dp", "expert"), "tensor"),
            P(("dp", "expert"), None, "tensor"),
            P(("dp", "expert"), None, "tensor"),
            P("tensor", "dp"),
            P(("dp", "expert"), None),
            P(),
            P(("dp", "expert"), None),
            P(("dp", "expert"), None),
            P(("dp", "expert"), None, "tensor"),
            P(("dp", "expert"), None, "tensor"),
            P(("dp", "expert"), "tensor", None),
        ),
        out_specs=P(("dp", "expert"), "tensor"),
        check_vma=False,
    )
```

```python
import jax
import jax.numpy as jnp
from jax import lax
from jax.sharding import PartitionSpec as P

D = 2048
HEAD_WIDTH = 128
CAP = 6


def attend_local(queries, fresh_keys, fresh_values, resident_keys, resident_values):
    tokens_here = queries.shape[0]
    kv_here = fresh_keys.shape[1] // HEAD_WIDTH
    query_group = queries.shape[1] // HEAD_WIDTH // kv_here
    context = resident_keys.shape[1]
    query_rows = queries.reshape(tokens_here, kv_here, query_group, HEAD_WIDTH)
    joined_keys = jnp.concatenate([resident_keys[0], fresh_keys], 0).reshape(
        context + tokens_here, kv_here, HEAD_WIDTH
    )
    joined_values = jnp.concatenate([resident_values[0], fresh_values], 0).reshape(
        context + tokens_here, kv_here, HEAD_WIDTH
    )
    score = jnp.einsum(
        "tjgd,sjd->jgts", query_rows, joined_keys, preferred_element_type=jnp.float32
    ) * HEAD_WIDTH ** (-0.5)
    places = jnp.arange(context + tokens_here)
    rows = jnp.arange(tokens_here)
    allowed = (places[None, :] < context) | (places[None, :] - context <= rows[:, None])
    score = jnp.where(allowed, score, jnp.float32(-1e30))
    top_score = jnp.max(score, axis=-1, keepdims=True)
    weight = jnp.exp(score - top_score)
    probs = (weight / jnp.sum(weight, axis=-1, keepdims=True)).astype(jnp.bfloat16)
    attended = jnp.einsum(
        "jgts,sjd->tjgd", probs, joined_values, preferred_element_type=jnp.float32
    )
    return attended.reshape(tokens_here, -1).astype(jnp.bfloat16)


def swap_pair(x):
    return lax.ppermute(x, "tensor", [(0, 1), (1, 0)])


def per_device(
    queries,
    fresh_keys,
    fresh_values,
    resident_keys,
    resident_values,
    out_weight,
    residual,
    norm_gain,
    expert_ids,
    gates,
    w_gate,
    w_up,
    w_down,
):
    tokens_here = residual.shape[0]
    lane = lax.axis_index("tensor")
    half = D // lax.axis_size("tensor")
    groups = lax.axis_size("dp")
    attended = attend_local(queries, fresh_keys, fresh_values, resident_keys, resident_values)

    here = lax.axis_index("dp")
    blocks = [jnp.dot(attended, out_weight, preferred_element_type=jnp.float32)]
    for shift in range(1, groups):
        onward = [(i, (i + shift) % groups) for i in range(groups)]
        backward = [(i, (i - shift) % groups) for i in range(groups)]
        arrived = lax.ppermute(attended, "dp", onward)
        product = jnp.dot(arrived, out_weight, preferred_element_type=jnp.float32)
        blocks.append(lax.ppermute(product, "dp", backward))
    stacked = jnp.stack(blocks)
    order = (jnp.arange(groups) - here) % groups
    mine = stacked[order].transpose(1, 0, 2).reshape(tokens_here, D)
    summed = mine + swap_pair(mine)
    hidden = residual.astype(jnp.float32) + summed
    mean_square = jnp.mean(hidden * hidden, axis=-1, keepdims=True)
    normed = (hidden * lax.rsqrt(mean_square + 1e-06) * norm_gain).astype(jnp.bfloat16)
    hidden_half = lax.dynamic_slice_in_dim(hidden, lane * half, half, 1)
    normed_half = lax.dynamic_slice_in_dim(normed, lane * half, half, 1)

    owners = lax.axis_size("dp") * lax.axis_size("expert")
    onehot = (expert_ids[:, :, None] == jnp.arange(owners)[None, None, :]).astype(jnp.int32)
    per_token = jnp.sum(onehot, axis=1)
    before = jnp.cumsum(per_token, axis=0) - per_token
    slot = jnp.sum(onehot * before[:, None, :], axis=-1)
    code = expert_ids * CAP + slot
    pick = (code[:, :, None] == jnp.arange(owners * CAP)[None, None, :]).astype(jnp.bfloat16)
    spread = jnp.sum(pick, axis=1)
    lanes = 128
    width = half // lanes
    outgoing = jnp.einsum(
        "tr,tjl->rjl", spread, normed_half.reshape(tokens_here, width, lanes),
        preferred_element_type=jnp.float32,
    ).astype(jnp.bfloat16)
    received = lax.all_to_all(
        outgoing.reshape(owners, CAP * width, lanes), ("dp", "expert"), split_axis=0, concat_axis=0, tiled=True
    ).reshape(owners * CAP, width, lanes)
    other = swap_pair(received)
    first = jnp.where(lane == 0, received, other)
    second = jnp.where(lane == 0, other, received)
    flat = jnp.concatenate([first, second], axis=1)

    gate_part = jnp.einsum(
        "rjl,jlh->rh", flat, w_gate[0].reshape(2 * width, lanes, -1), preferred_element_type=jnp.float32
    )
    up_part = jnp.einsum(
        "rjl,jlh->rh", flat, w_up[0].reshape(2 * width, lanes, -1), preferred_element_type=jnp.float32
    )
    act = (jax.nn.silu(gate_part) * up_part).astype(jnp.bfloat16)
    result = jnp.einsum(
        "rh,hjl->rjl", act, w_down[0].reshape(act.shape[1], 2 * width, lanes), preferred_element_type=jnp.float32
    )
    own = lax.dynamic_slice_in_dim(result, lane * width, width, 1)
    theirs = lax.dynamic_slice_in_dim(result, (1 - lane) * width, width, 1)
    expert_out = (own + swap_pair(theirs)).astype(jnp.bfloat16)

    returned = lax.all_to_all(
        expert_out.reshape(owners, CAP * width, lanes), ("dp", "expert"), split_axis=0, concat_axis=0, tiled=True
    ).reshape(owners * CAP, width, lanes)
    picked = jnp.einsum("tkr,rjl->tkjl", pick, returned, preferred_element_type=jnp.float32)
    moe = jnp.sum(gates[:, :, None, None] * picked, axis=1).reshape(tokens_here, half)
    return (hidden_half + moe).astype(jnp.bfloat16)


def solution(mesh):
    return jax.shard_map(
        per_device,
        mesh=mesh,
        in_specs=(
            P(("dp", "expert"), "tensor"),
            P(("dp", "expert"), "tensor"),
            P(("dp", "expert"), "tensor"),
            P(("dp", "expert"), None, "tensor"),
            P(("dp", "expert"), None, "tensor"),
            P("tensor", "dp"),
            P(("dp", "expert"), None),
            P(),
            P(("dp", "expert"), None),
            P(("dp", "expert"), None),
            P(("dp", "expert"), None, "tensor"),
            P(("dp", "expert"), None, "tensor"),
            P(("dp", "expert"), "tensor", None),
        ),
        out_specs=P(("dp", "expert"), "tensor"),
        check_vma=False,
    )
```

```python
import jax
import jax.numpy as jnp
from jax import lax
from jax.experimental import pallas as pl
from jax.sharding import PartitionSpec as P

D = 2048
HEAD_WIDTH = 128
CAP = 6


def attend_local(queries, fresh_keys, fresh_values, resident_keys, resident_values):
    tokens_here = queries.shape[0]
    kv_here = fresh_keys.shape[1] // HEAD_WIDTH
    query_group = queries.shape[1] // HEAD_WIDTH // kv_here
    context = resident_keys.shape[1]
    query_rows = queries.reshape(tokens_here, kv_here, query_group, HEAD_WIDTH)
    joined_keys = jnp.concatenate([resident_keys[0], fresh_keys], 0).reshape(
        context + tokens_here, kv_here, HEAD_WIDTH
    )
    joined_values = jnp.concatenate([resident_values[0], fresh_values], 0).reshape(
        context + tokens_here, kv_here, HEAD_WIDTH
    )
    score = jnp.einsum(
        "tjgd,sjd->jgts", query_rows, joined_keys, preferred_element_type=jnp.float32
    ) * HEAD_WIDTH ** (-0.5)
    places = jnp.arange(context + tokens_here)
    rows = jnp.arange(tokens_here)
    allowed = (places[None, :] < context) | (places[None, :] - context <= rows[:, None])
    score = jnp.where(allowed, score, jnp.float32(-1e30))
    top_score = jnp.max(score, axis=-1, keepdims=True)
    weight = jnp.exp(score - top_score)
    probs = (weight / jnp.sum(weight, axis=-1, keepdims=True)).astype(jnp.bfloat16)
    attended = jnp.einsum(
        "jgts,sjd->tjgd", probs, joined_values, preferred_element_type=jnp.float32
    )
    return attended.reshape(tokens_here, -1).astype(jnp.bfloat16)


def attention_kernel(q_ref, kn_ref, vn_ref, kr_ref, vr_ref, o_ref):
    tokens = q_ref.shape[0]
    group = q_ref.shape[1] // HEAD_WIDTH
    k_res = kr_ref[0]
    v_res = vr_ref[0]
    k_new = kn_ref[...]
    v_new = vn_ref[...]
    rows = lax.broadcasted_iota(jnp.int32, (tokens, tokens), 0)
    cols = lax.broadcasted_iota(jnp.int32, (tokens, tokens), 1)
    visible = cols <= rows
    scale = HEAD_WIDTH ** (-0.5)
    dims = (((1,), (1,)), ((), ()))
    for g in range(group):
        q = q_ref[:, g * HEAD_WIDTH:(g + 1) * HEAD_WIDTH]
        s_res = lax.dot_general(q, k_res, dims, preferred_element_type=jnp.float32) * scale
        s_new = lax.dot_general(q, k_new, dims, preferred_element_type=jnp.float32) * scale
        s_new = jnp.where(visible, s_new, jnp.float32(-1e30))
        top = jnp.maximum(
            jnp.max(s_res, axis=1, keepdims=True), jnp.max(s_new, axis=1, keepdims=True)
        )
        w_res = jnp.exp(s_res - top)
        w_new = jnp.exp(s_new - top)
        total = jnp.sum(w_res, axis=1, keepdims=True) + jnp.sum(w_new, axis=1, keepdims=True)
        p_res = (w_res / total).astype(jnp.bfloat16)
        p_new = (w_new / total).astype(jnp.bfloat16)
        out = jnp.dot(p_res, v_res, preferred_element_type=jnp.float32) + jnp.dot(
            p_new, v_new, preferred_element_type=jnp.float32
        )
        o_ref[:, g * HEAD_WIDTH:(g + 1) * HEAD_WIDTH] = out.astype(o_ref.dtype)


def attend_kernel(queries, fresh_keys, fresh_values, resident_keys, resident_values, interpret=False):
    tokens = queries.shape[0]
    kv_here = fresh_keys.shape[1] // HEAD_WIDTH
    width = queries.shape[1] // kv_here
    context = resident_keys.shape[1]
    return pl.pallas_call(
        attention_kernel,
        grid=(kv_here,),
        in_specs=[
            pl.BlockSpec((tokens, width), lambda j: (0, j)),
            pl.BlockSpec((tokens, HEAD_WIDTH), lambda j: (0, j)),
            pl.BlockSpec((tokens, HEAD_WIDTH), lambda j: (0, j)),
            pl.BlockSpec((1, context, HEAD_WIDTH), lambda j: (0, 0, j)),
            pl.BlockSpec((1, context, HEAD_WIDTH), lambda j: (0, 0, j)),
        ],
        out_specs=pl.BlockSpec((tokens, width), lambda j: (0, j)),
        out_shape=jax.ShapeDtypeStruct(queries.shape, jnp.bfloat16),
        interpret=interpret,
    )(queries, fresh_keys, fresh_values, resident_keys, resident_values)


def swap_pair(x):
    return lax.ppermute(x, "tensor", [(0, 1), (1, 0)])


def per_device(
    queries,
    fresh_keys,
    fresh_values,
    resident_keys,
    resident_values,
    out_weight,
    residual,
    norm_gain,
    expert_ids,
    gates,
    w_gate,
    w_up,
    w_down,
):
    tokens_here = residual.shape[0]
    lane = lax.axis_index("tensor")
    half = D // lax.axis_size("tensor")
    groups = lax.axis_size("dp")
    attended = attend_kernel(queries, fresh_keys, fresh_values, resident_keys, resident_values)

    here = lax.axis_index("dp")
    blocks = [jnp.dot(attended, out_weight, preferred_element_type=jnp.float32)]
    for shift in range(1, groups):
        onward = [(i, (i + shift) % groups) for i in range(groups)]
        backward = [(i, (i - shift) % groups) for i in range(groups)]
        arrived = lax.ppermute(attended, "dp", onward)
        product = jnp.dot(arrived, out_weight, preferred_element_type=jnp.float32)
        blocks.append(lax.ppermute(product, "dp", backward))
    stacked = jnp.stack(blocks)
    order = (jnp.arange(groups) - here) % groups
    mine = stacked[order].transpose(1, 0, 2).reshape(tokens_here, D)
    summed = mine + swap_pair(mine)
    hidden = residual.astype(jnp.float32) + summed
    mean_square = jnp.mean(hidden * hidden, axis=-1, keepdims=True)
    normed = (hidden * lax.rsqrt(mean_square + 1e-06) * norm_gain).astype(jnp.bfloat16)
    hidden_half = lax.dynamic_slice_in_dim(hidden, lane * half, half, 1)
    normed_half = lax.dynamic_slice_in_dim(normed, lane * half, half, 1)

    owners = lax.axis_size("dp") * lax.axis_size("expert")
    onehot = (expert_ids[:, :, None] == jnp.arange(owners)[None, None, :]).astype(jnp.int32)
    per_token = jnp.sum(onehot, axis=1)
    before = jnp.cumsum(per_token, axis=0) - per_token
    slot = jnp.sum(onehot * before[:, None, :], axis=-1)
    code = expert_ids * CAP + slot
    pick = (code[:, :, None] == jnp.arange(owners * CAP)[None, None, :]).astype(jnp.bfloat16)
    spread = jnp.sum(pick, axis=1)
    lanes = 128
    width = half // lanes
    outgoing = jnp.einsum(
        "tr,tjl->rjl", spread, normed_half.reshape(tokens_here, width, lanes),
        preferred_element_type=jnp.float32,
    ).astype(jnp.bfloat16)
    received = lax.all_to_all(
        outgoing.reshape(owners, CAP * width, lanes), ("dp", "expert"), split_axis=0, concat_axis=0, tiled=True
    ).reshape(owners * CAP, width, lanes)
    other = swap_pair(received)
    first = jnp.where(lane == 0, received, other)
    second = jnp.where(lane == 0, other, received)
    flat = jnp.concatenate([first, second], axis=1)

    gate_part = jnp.einsum(
        "rjl,jlh->rh", flat, w_gate[0].reshape(2 * width, lanes, -1), preferred_element_type=jnp.float32
    )
    up_part = jnp.einsum(
        "rjl,jlh->rh", flat, w_up[0].reshape(2 * width, lanes, -1), preferred_element_type=jnp.float32
    )
    act = (jax.nn.silu(gate_part) * up_part).astype(jnp.bfloat16)
    result = jnp.einsum(
        "rh,hjl->rjl", act, w_down[0].reshape(act.shape[1], 2 * width, lanes), preferred_element_type=jnp.float32
    )
    own = lax.dynamic_slice_in_dim(result, lane * width, width, 1)
    theirs = lax.dynamic_slice_in_dim(result, (1 - lane) * width, width, 1)
    expert_out = (own + swap_pair(theirs)).astype(jnp.bfloat16)

    returned = lax.all_to_all(
        expert_out.reshape(owners, CAP * width, lanes), ("dp", "expert"), split_axis=0, concat_axis=0, tiled=True
    ).reshape(owners * CAP, width, lanes)
    picked = jnp.einsum("tkr,rjl->tkjl", pick, returned, preferred_element_type=jnp.float32)
    moe = jnp.sum(gates[:, :, None, None] * picked, axis=1).reshape(tokens_here, half)
    return (hidden_half + moe).astype(jnp.bfloat16)


def solution(mesh):
    return jax.shard_map(
        per_device,
        mesh=mesh,
        in_specs=(
            P(("dp", "expert"), "tensor"),
            P(("dp", "expert"), "tensor"),
            P(("dp", "expert"), "tensor"),
            P(("dp", "expert"), None, "tensor"),
            P(("dp", "expert"), None, "tensor"),
            P("tensor", "dp"),
            P(("dp", "expert"), None),
            P(),
            P(("dp", "expert"), None),
            P(("dp", "expert"), None),
            P(("dp", "expert"), None, "tensor"),
            P(("dp", "expert"), None, "tensor"),
            P(("dp", "expert"), "tensor", None),
        ),
        out_specs=P(("dp", "expert"), "tensor"),
        check_vma=False,
    )
```

```python
import jax
import jax.numpy as jnp
from jax import lax
from jax.experimental import pallas as pl
from jax.experimental.pallas import tpu as pltpu
from jax.sharding import PartitionSpec as P

D = 2048
HEAD_WIDTH = 128
CAP = 6


def attend_local(queries, fresh_keys, fresh_values, resident_keys, resident_values):
    tokens_here = queries.shape[0]
    kv_here = fresh_keys.shape[1] // HEAD_WIDTH
    query_group = queries.shape[1] // HEAD_WIDTH // kv_here
    context = resident_keys.shape[1]
    query_rows = queries.reshape(tokens_here, kv_here, query_group, HEAD_WIDTH)
    joined_keys = jnp.concatenate([resident_keys[0], fresh_keys], 0).reshape(
        context + tokens_here, kv_here, HEAD_WIDTH
    )
    joined_values = jnp.concatenate([resident_values[0], fresh_values], 0).reshape(
        context + tokens_here, kv_here, HEAD_WIDTH
    )
    score = jnp.einsum(
        "tjgd,sjd->jgts", query_rows, joined_keys, preferred_element_type=jnp.float32
    ) * HEAD_WIDTH ** (-0.5)
    places = jnp.arange(context + tokens_here)
    rows = jnp.arange(tokens_here)
    allowed = (places[None, :] < context) | (places[None, :] - context <= rows[:, None])
    score = jnp.where(allowed, score, jnp.float32(-1e30))
    top_score = jnp.max(score, axis=-1, keepdims=True)
    weight = jnp.exp(score - top_score)
    probs = (weight / jnp.sum(weight, axis=-1, keepdims=True)).astype(jnp.bfloat16)
    attended = jnp.einsum(
        "jgts,sjd->tjgd", probs, joined_values, preferred_element_type=jnp.float32
    )
    return attended.reshape(tokens_here, -1).astype(jnp.bfloat16)


def attention_kernel(q_ref, kn_ref, vn_ref, kr_ref, vr_ref, o_ref):
    tokens = q_ref.shape[0]
    group = q_ref.shape[1] // HEAD_WIDTH
    k_res = kr_ref[0]
    v_res = vr_ref[0]
    k_new = kn_ref[...]
    v_new = vn_ref[...]
    rows = lax.broadcasted_iota(jnp.int32, (tokens, tokens), 0)
    cols = lax.broadcasted_iota(jnp.int32, (tokens, tokens), 1)
    visible = cols <= rows
    scale = HEAD_WIDTH ** (-0.5)
    dims = (((1,), (1,)), ((), ()))
    for g in range(group):
        q = q_ref[:, g * HEAD_WIDTH:(g + 1) * HEAD_WIDTH]
        s_res = lax.dot_general(q, k_res, dims, preferred_element_type=jnp.float32) * scale
        s_new = lax.dot_general(q, k_new, dims, preferred_element_type=jnp.float32) * scale
        s_new = jnp.where(visible, s_new, jnp.float32(-1e30))
        top = jnp.maximum(
            jnp.max(s_res, axis=1, keepdims=True), jnp.max(s_new, axis=1, keepdims=True)
        )
        w_res = jnp.exp(s_res - top)
        w_new = jnp.exp(s_new - top)
        total = jnp.sum(w_res, axis=1, keepdims=True) + jnp.sum(w_new, axis=1, keepdims=True)
        p_res = (w_res / total).astype(jnp.bfloat16)
        p_new = (w_new / total).astype(jnp.bfloat16)
        out = jnp.dot(p_res, v_res, preferred_element_type=jnp.float32) + jnp.dot(
            p_new, v_new, preferred_element_type=jnp.float32
        )
        o_ref[:, g * HEAD_WIDTH:(g + 1) * HEAD_WIDTH] = out.astype(o_ref.dtype)


def attend_kernel(queries, fresh_keys, fresh_values, resident_keys, resident_values, interpret=False):
    tokens = queries.shape[0]
    kv_here = fresh_keys.shape[1] // HEAD_WIDTH
    width = queries.shape[1] // kv_here
    context = resident_keys.shape[1]
    return pl.pallas_call(
        attention_kernel,
        grid=(kv_here,),
        in_specs=[
            pl.BlockSpec((tokens, width), lambda j: (0, j)),
            pl.BlockSpec((tokens, HEAD_WIDTH), lambda j: (0, j)),
            pl.BlockSpec((tokens, HEAD_WIDTH), lambda j: (0, j)),
            pl.BlockSpec((1, context, HEAD_WIDTH), lambda j: (0, 0, j)),
            pl.BlockSpec((1, context, HEAD_WIDTH), lambda j: (0, 0, j)),
        ],
        out_specs=pl.BlockSpec((tokens, width), lambda j: (0, j)),
        out_shape=jax.ShapeDtypeStruct(queries.shape, jnp.bfloat16),
        interpret=interpret,
    )(queries, fresh_keys, fresh_values, resident_keys, resident_values)


def expert_kernel(lane_ref, mine_ref, other_ref, g_own, g_other, u_own, u_other, d_own, d_other, own_ref, theirs_ref):
    fold = g_own.shape[0] // HEAD_WIDTH
    rows = own_ref.shape[0] // fold
    gate = jnp.zeros((rows, g_own.shape[1]), jnp.float32)
    up = jnp.zeros((rows, g_own.shape[1]), jnp.float32)
    for j in range(fold):
        part = pl.ds(j * HEAD_WIDTH, HEAD_WIDTH)
        x_mine = mine_ref[pl.ds(j, rows, stride=fold), :]
        x_other = other_ref[pl.ds(j, rows, stride=fold), :]
        gate = gate + jnp.dot(x_mine, g_own[part, :], preferred_element_type=jnp.float32)
        gate = gate + jnp.dot(x_other, g_other[part, :], preferred_element_type=jnp.float32)
        up = up + jnp.dot(x_mine, u_own[part, :], preferred_element_type=jnp.float32)
        up = up + jnp.dot(x_other, u_other[part, :], preferred_element_type=jnp.float32)
    act = (gate / (1.0 + jnp.exp(-gate)) * up).astype(jnp.bfloat16)
    for j in range(fold):
        part = pl.ds(j * HEAD_WIDTH, HEAD_WIDTH)
        own_ref[pl.ds(j, rows, stride=fold), :] = jnp.dot(
            act, d_own[:, part], preferred_element_type=jnp.float32
        )
        theirs_ref[pl.ds(j, rows, stride=fold), :] = jnp.dot(
            act, d_other[:, part], preferred_element_type=jnp.float32
        )


def expert_ffn(lane, mine, other, gate_mat, up_mat, down_mat, block_rows=256, interpret=False):
    folded, lanes = mine.shape
    half, hidden = gate_mat.shape[0] // 2, gate_mat.shape[1]
    fold = half // lanes
    rows = folded // fold
    step = block_rows * fold
    act_spec = pl.BlockSpec((step, lanes), lambda i, lane_ref: (i, 0))
    own_rows = pl.BlockSpec((half, hidden), lambda i, lane_ref: (lane_ref[0], 0))
    other_rows = pl.BlockSpec((half, hidden), lambda i, lane_ref: (1 - lane_ref[0], 0))
    own_cols = pl.BlockSpec((hidden, half), lambda i, lane_ref: (0, lane_ref[0]))
    other_cols = pl.BlockSpec((hidden, half), lambda i, lane_ref: (0, 1 - lane_ref[0]))
    return pl.pallas_call(
        expert_kernel,
        grid_spec=pltpu.PrefetchScalarGridSpec(
            num_scalar_prefetch=1,
            grid=(rows // block_rows,),
            in_specs=[act_spec, act_spec, own_rows, other_rows, own_rows, other_rows, own_cols, other_cols],
            out_specs=[act_spec, act_spec],
        ),
        out_shape=[
            jax.ShapeDtypeStruct((folded, lanes), jnp.float32),
            jax.ShapeDtypeStruct((folded, lanes), jnp.float32),
        ],
        interpret=interpret,
    )(lane, mine, other, gate_mat, gate_mat, up_mat, up_mat, down_mat, down_mat)


def swap_pair(x):
    return lax.ppermute(x, "tensor", [(0, 1), (1, 0)])


def per_device(
    queries,
    fresh_keys,
    fresh_values,
    resident_keys,
    resident_values,
    out_weight,
    residual,
    norm_gain,
    expert_ids,
    gates,
    w_gate,
    w_up,
    w_down,
):
    tokens_here = residual.shape[0]
    lane = lax.axis_index("tensor")
    half = D // lax.axis_size("tensor")
    groups = lax.axis_size("dp")
    attended = attend_kernel(queries, fresh_keys, fresh_values, resident_keys, resident_values)

    here = lax.axis_index("dp")
    blocks = [jnp.dot(attended, out_weight, preferred_element_type=jnp.float32)]
    for shift in range(1, groups):
        onward = [(i, (i + shift) % groups) for i in range(groups)]
        backward = [(i, (i - shift) % groups) for i in range(groups)]
        arrived = lax.ppermute(attended, "dp", onward)
        product = jnp.dot(arrived, out_weight, preferred_element_type=jnp.float32)
        blocks.append(lax.ppermute(product, "dp", backward))
    stacked = jnp.stack(blocks)
    order = (jnp.arange(groups) - here) % groups
    mine = stacked[order].transpose(1, 0, 2).reshape(tokens_here, D)
    summed = mine + swap_pair(mine)
    hidden = residual.astype(jnp.float32) + summed
    mean_square = jnp.mean(hidden * hidden, axis=-1, keepdims=True)
    normed = (hidden * lax.rsqrt(mean_square + 1e-06) * norm_gain).astype(jnp.bfloat16)
    hidden_half = lax.dynamic_slice_in_dim(hidden, lane * half, half, 1)
    normed_half = lax.dynamic_slice_in_dim(normed, lane * half, half, 1)

    owners = lax.axis_size("dp") * lax.axis_size("expert")
    onehot = (expert_ids[:, :, None] == jnp.arange(owners)[None, None, :]).astype(jnp.int32)
    per_token = jnp.sum(onehot, axis=1)
    before = jnp.cumsum(per_token, axis=0) - per_token
    slot = jnp.sum(onehot * before[:, None, :], axis=-1)
    code = expert_ids * CAP + slot
    pick = (code[:, :, None] == jnp.arange(owners * CAP)[None, None, :]).astype(jnp.bfloat16)
    spread = jnp.sum(pick, axis=1)
    lanes = 128
    width = half // lanes
    outgoing = jnp.einsum(
        "tr,tjl->rjl", spread, normed_half.reshape(tokens_here, width, lanes),
        preferred_element_type=jnp.float32,
    ).astype(jnp.bfloat16)
    received = lax.all_to_all(
        outgoing.reshape(owners, CAP * width, lanes), ("dp", "expert"), split_axis=0, concat_axis=0, tiled=True
    ).reshape(owners * CAP * width, lanes)
    other = swap_pair(received)
    own, theirs = expert_ffn(
        lane.astype(jnp.int32).reshape(1), received, other, w_gate[0], w_up[0], w_down[0]
    )
    expert_out = (own + swap_pair(theirs.astype(jnp.bfloat16)).astype(jnp.float32)).astype(jnp.bfloat16)

    returned = lax.all_to_all(
        expert_out.reshape(owners, CAP * width, lanes), ("dp", "expert"), split_axis=0, concat_axis=0, tiled=True
    ).reshape(owners * CAP, width, lanes)
    picked = jnp.einsum("tkr,rjl->tkjl", pick, returned, preferred_element_type=jnp.float32)
    moe = jnp.sum(gates[:, :, None, None] * picked, axis=1).reshape(tokens_here, half)
    return (hidden_half + moe).astype(jnp.bfloat16)


def solution(mesh):
    return jax.shard_map(
        per_device,
        mesh=mesh,
        in_specs=(
            P(("dp", "expert"), "tensor"),
            P(("dp", "expert"), "tensor"),
            P(("dp", "expert"), "tensor"),
            P(("dp", "expert"), None, "tensor"),
            P(("dp", "expert"), None, "tensor"),
            P("tensor", "dp"),
            P(("dp", "expert"), None),
            P(),
            P(("dp", "expert"), None),
            P(("dp", "expert"), None),
            P(("dp", "expert"), None, "tensor"),
            P(("dp", "expert"), None, "tensor"),
            P(("dp", "expert"), "tensor", None),
        ),
        out_specs=P(("dp", "expert"), "tensor"),
        check_vma=False,
    )
```

```python
import jax
import jax.numpy as jnp
from jax import lax
from jax.experimental import pallas as pl
from jax.experimental.pallas import tpu as pltpu
from jax.sharding import PartitionSpec as P

D = 2048
HEAD_WIDTH = 128
CAP = 6


def attend_local(queries, fresh_keys, fresh_values, resident_keys, resident_values):
    tokens_here = queries.shape[0]
    kv_here = fresh_keys.shape[1] // HEAD_WIDTH
    query_group = queries.shape[1] // HEAD_WIDTH // kv_here
    context = resident_keys.shape[1]
    query_rows = queries.reshape(tokens_here, kv_here, query_group, HEAD_WIDTH)
    joined_keys = jnp.concatenate([resident_keys[0], fresh_keys], 0).reshape(
        context + tokens_here, kv_here, HEAD_WIDTH
    )
    joined_values = jnp.concatenate([resident_values[0], fresh_values], 0).reshape(
        context + tokens_here, kv_here, HEAD_WIDTH
    )
    score = jnp.einsum(
        "tjgd,sjd->jgts", query_rows, joined_keys, preferred_element_type=jnp.float32
    ) * HEAD_WIDTH ** (-0.5)
    places = jnp.arange(context + tokens_here)
    rows = jnp.arange(tokens_here)
    allowed = (places[None, :] < context) | (places[None, :] - context <= rows[:, None])
    score = jnp.where(allowed, score, jnp.float32(-1e30))
    top_score = jnp.max(score, axis=-1, keepdims=True)
    weight = jnp.exp(score - top_score)
    probs = (weight / jnp.sum(weight, axis=-1, keepdims=True)).astype(jnp.bfloat16)
    attended = jnp.einsum(
        "jgts,sjd->tjgd", probs, joined_values, preferred_element_type=jnp.float32
    )
    return attended.reshape(tokens_here, -1).astype(jnp.bfloat16)


def attention_kernel(q_ref, kn_ref, vn_ref, kr_ref, vr_ref, o_ref):
    tokens = q_ref.shape[0]
    group = q_ref.shape[1] // HEAD_WIDTH
    k_res = kr_ref[0]
    v_res = vr_ref[0]
    k_new = kn_ref[...]
    v_new = vn_ref[...]
    rows = lax.broadcasted_iota(jnp.int32, (tokens, tokens), 0)
    cols = lax.broadcasted_iota(jnp.int32, (tokens, tokens), 1)
    visible = cols <= rows
    scale = HEAD_WIDTH ** (-0.5)
    dims = (((1,), (1,)), ((), ()))
    for g in range(group):
        q = q_ref[:, g * HEAD_WIDTH:(g + 1) * HEAD_WIDTH]
        s_res = lax.dot_general(q, k_res, dims, preferred_element_type=jnp.float32) * scale
        s_new = lax.dot_general(q, k_new, dims, preferred_element_type=jnp.float32) * scale
        s_new = jnp.where(visible, s_new, jnp.float32(-1e30))
        top = jnp.maximum(
            jnp.max(s_res, axis=1, keepdims=True), jnp.max(s_new, axis=1, keepdims=True)
        )
        w_res = jnp.exp(s_res - top)
        w_new = jnp.exp(s_new - top)
        total = jnp.sum(w_res, axis=1, keepdims=True) + jnp.sum(w_new, axis=1, keepdims=True)
        p_res = (w_res / total).astype(jnp.bfloat16)
        p_new = (w_new / total).astype(jnp.bfloat16)
        out = jnp.dot(p_res, v_res, preferred_element_type=jnp.float32) + jnp.dot(
            p_new, v_new, preferred_element_type=jnp.float32
        )
        o_ref[:, g * HEAD_WIDTH:(g + 1) * HEAD_WIDTH] = out.astype(o_ref.dtype)


def attend_kernel(queries, fresh_keys, fresh_values, resident_keys, resident_values, interpret=False):
    tokens = queries.shape[0]
    kv_here = fresh_keys.shape[1] // HEAD_WIDTH
    width = queries.shape[1] // kv_here
    context = resident_keys.shape[1]
    return pl.pallas_call(
        attention_kernel,
        grid=(kv_here,),
        in_specs=[
            pl.BlockSpec((tokens, width), lambda j: (0, j)),
            pl.BlockSpec((tokens, HEAD_WIDTH), lambda j: (0, j)),
            pl.BlockSpec((tokens, HEAD_WIDTH), lambda j: (0, j)),
            pl.BlockSpec((1, context, HEAD_WIDTH), lambda j: (0, 0, j)),
            pl.BlockSpec((1, context, HEAD_WIDTH), lambda j: (0, 0, j)),
        ],
        out_specs=pl.BlockSpec((tokens, width), lambda j: (0, j)),
        out_shape=jax.ShapeDtypeStruct(queries.shape, jnp.bfloat16),
        interpret=interpret,
    )(queries, fresh_keys, fresh_values, resident_keys, resident_values)


def gate_up_kernel(lane_ref, mine_ref, other_ref, g_own, g_other, u_own, u_other, act_ref):
    fold = g_own.shape[0] // HEAD_WIDTH
    rows = act_ref.shape[0]
    x_mine = jnp.concatenate(
        [mine_ref[pl.ds(j, rows, stride=fold), :] for j in range(fold)], axis=1
    )
    x_other = jnp.concatenate(
        [other_ref[pl.ds(j, rows, stride=fold), :] for j in range(fold)], axis=1
    )
    gate = jnp.dot(x_mine, g_own[...], preferred_element_type=jnp.float32) + jnp.dot(
        x_other, g_other[...], preferred_element_type=jnp.float32
    )
    up = jnp.dot(x_mine, u_own[...], preferred_element_type=jnp.float32) + jnp.dot(
        x_other, u_other[...], preferred_element_type=jnp.float32
    )
    act_ref[...] = (gate / (1.0 + jnp.exp(-gate)) * up).astype(act_ref.dtype)


def down_kernel(lane_ref, act_mine, act_other, d_own, d_other, out_ref):
    fold = d_own.shape[1] // HEAD_WIDTH
    rows = act_mine.shape[0]
    out = jnp.dot(act_mine[...], d_own[...], preferred_element_type=jnp.float32) + jnp.dot(
        act_other[...], d_other[...], preferred_element_type=jnp.float32
    )
    for j in range(fold):
        out_ref[pl.ds(j, rows, stride=fold), :] = out[:, j * HEAD_WIDTH:(j + 1) * HEAD_WIDTH]


def gate_up(lane, mine, other, gate_mat, up_mat, block_rows=256, interpret=False):
    folded, lanes = mine.shape
    half, hidden = gate_mat.shape[0] // 2, gate_mat.shape[1]
    fold = half // lanes
    rows = folded // fold
    act_spec = pl.BlockSpec((block_rows * fold, lanes), lambda i, lane_ref: (i, 0))
    own_rows = pl.BlockSpec((half, hidden), lambda i, lane_ref: (lane_ref[0], 0))
    other_rows = pl.BlockSpec((half, hidden), lambda i, lane_ref: (1 - lane_ref[0], 0))
    return pl.pallas_call(
        gate_up_kernel,
        grid_spec=pltpu.PrefetchScalarGridSpec(
            num_scalar_prefetch=1,
            grid=(rows // block_rows,),
            in_specs=[act_spec, act_spec, own_rows, other_rows, own_rows, other_rows],
            out_specs=pl.BlockSpec((block_rows, hidden), lambda i, lane_ref: (i, 0)),
        ),
        out_shape=jax.ShapeDtypeStruct((rows, hidden), jnp.bfloat16),
        interpret=interpret,
    )(lane, mine, other, gate_mat, gate_mat, up_mat, up_mat)


def down(lane, act_mine, act_other, down_mat, down_other, block_rows=256, interpret=False):
    rows, hidden = act_mine.shape
    half = down_other.shape[1]
    fold = half // HEAD_WIDTH
    act_spec = pl.BlockSpec((block_rows, hidden), lambda i, lane_ref: (i, 0))
    return pl.pallas_call(
        down_kernel,
        grid_spec=pltpu.PrefetchScalarGridSpec(
            num_scalar_prefetch=1,
            grid=(rows // block_rows,),
            in_specs=[
                act_spec,
                act_spec,
                pl.BlockSpec((hidden, half), lambda i, lane_ref: (0, lane_ref[0])),
                pl.BlockSpec((hidden, half), lambda i, lane_ref: (0, 0)),
            ],
            out_specs=pl.BlockSpec((block_rows * fold, HEAD_WIDTH), lambda i, lane_ref: (i, 0)),
        ),
        out_shape=jax.ShapeDtypeStruct((rows * fold, HEAD_WIDTH), jnp.float32),
        interpret=interpret,
    )(lane, act_mine, act_other, down_mat, down_other)


def swap_pair(x):
    return lax.ppermute(x, "tensor", [(0, 1), (1, 0)])


def per_device(
    queries,
    fresh_keys,
    fresh_values,
    resident_keys,
    resident_values,
    out_weight,
    residual,
    norm_gain,
    expert_ids,
    gates,
    w_gate,
    w_up,
    w_down,
):
    tokens_here = residual.shape[0]
    lane = lax.axis_index("tensor")
    half = D // lax.axis_size("tensor")
    groups = lax.axis_size("dp")
    attended = attend_kernel(queries, fresh_keys, fresh_values, resident_keys, resident_values)

    here = lax.axis_index("dp")
    blocks = [jnp.dot(attended, out_weight, preferred_element_type=jnp.float32)]
    for shift in range(1, groups):
        onward = [(i, (i + shift) % groups) for i in range(groups)]
        backward = [(i, (i - shift) % groups) for i in range(groups)]
        arrived = lax.ppermute(attended, "dp", onward)
        product = jnp.dot(arrived, out_weight, preferred_element_type=jnp.float32)
        blocks.append(lax.ppermute(product, "dp", backward))
    stacked = jnp.stack(blocks)
    order = (jnp.arange(groups) - here) % groups
    mine = stacked[order].transpose(1, 0, 2).reshape(tokens_here, D)
    summed = mine + swap_pair(mine)
    hidden = residual.astype(jnp.float32) + summed
    mean_square = jnp.mean(hidden * hidden, axis=-1, keepdims=True)
    normed = (hidden * lax.rsqrt(mean_square + 1e-06) * norm_gain).astype(jnp.bfloat16)
    hidden_half = lax.dynamic_slice_in_dim(hidden, lane * half, half, 1)
    normed_half = lax.dynamic_slice_in_dim(normed, lane * half, half, 1)

    owners = lax.axis_size("dp") * lax.axis_size("expert")
    onehot = (expert_ids[:, :, None] == jnp.arange(owners)[None, None, :]).astype(jnp.int32)
    per_token = jnp.sum(onehot, axis=1)
    before = jnp.cumsum(per_token, axis=0) - per_token
    slot = jnp.sum(onehot * before[:, None, :], axis=-1)
    code = expert_ids * CAP + slot
    pick = (code[:, :, None] == jnp.arange(owners * CAP)[None, None, :]).astype(jnp.bfloat16)
    spread = jnp.sum(pick, axis=1)
    lanes = 128
    width = half // lanes
    outgoing = jnp.einsum(
        "tr,tjl->rjl", spread, normed_half.reshape(tokens_here, width, lanes),
        preferred_element_type=jnp.float32,
    ).astype(jnp.bfloat16)
    received = lax.all_to_all(
        outgoing.reshape(owners, CAP * width, lanes), ("dp", "expert"), split_axis=0, concat_axis=0, tiled=True
    ).reshape(owners * CAP * width, lanes)
    other = swap_pair(received)
    lane_id = lane.astype(jnp.int32).reshape(1)
    down_other = swap_pair(lax.dynamic_slice_in_dim(w_down[0], (1 - lane) * half, half, 1))
    act = gate_up(lane_id, received, other, w_gate[0], w_up[0])
    expert_out = down(lane_id, act, swap_pair(act), w_down[0], down_other).astype(jnp.bfloat16)

    returned = lax.all_to_all(
        expert_out.reshape(owners, CAP * width, lanes), ("dp", "expert"), split_axis=0, concat_axis=0, tiled=True
    ).reshape(owners * CAP, width, lanes)
    picked = jnp.einsum("tkr,rjl->tkjl", pick, returned, preferred_element_type=jnp.float32)
    moe = jnp.sum(gates[:, :, None, None] * picked, axis=1).reshape(tokens_here, half)
    return (hidden_half + moe).astype(jnp.bfloat16)


def solution(mesh):
    return jax.shard_map(
        per_device,
        mesh=mesh,
        in_specs=(
            P(("dp", "expert"), "tensor"),
            P(("dp", "expert"), "tensor"),
            P(("dp", "expert"), "tensor"),
            P(("dp", "expert"), None, "tensor"),
            P(("dp", "expert"), None, "tensor"),
            P("tensor", "dp"),
            P(("dp", "expert"), None),
            P(),
            P(("dp", "expert"), None),
            P(("dp", "expert"), None),
            P(("dp", "expert"), None, "tensor"),
            P(("dp", "expert"), None, "tensor"),
            P(("dp", "expert"), "tensor", None),
        ),
        out_specs=P(("dp", "expert"), "tensor"),
        check_vma=False,
    )
```

```python
import jax
import jax.numpy as jnp
from jax import lax
from jax.experimental import pallas as pl
from jax.experimental.pallas import tpu as pltpu
from jax.sharding import PartitionSpec as P

D = 2048
HEAD_WIDTH = 128
CAP = 6


def attend_local(queries, fresh_keys, fresh_values, resident_keys, resident_values):
    tokens_here = queries.shape[0]
    kv_here = fresh_keys.shape[1] // HEAD_WIDTH
    query_group = queries.shape[1] // HEAD_WIDTH // kv_here
    context = resident_keys.shape[1]
    query_rows = queries.reshape(tokens_here, kv_here, query_group, HEAD_WIDTH)
    joined_keys = jnp.concatenate([resident_keys[0], fresh_keys], 0).reshape(
        context + tokens_here, kv_here, HEAD_WIDTH
    )
    joined_values = jnp.concatenate([resident_values[0], fresh_values], 0).reshape(
        context + tokens_here, kv_here, HEAD_WIDTH
    )
    score = jnp.einsum(
        "tjgd,sjd->jgts", query_rows, joined_keys, preferred_element_type=jnp.float32
    ) * HEAD_WIDTH ** (-0.5)
    places = jnp.arange(context + tokens_here)
    rows = jnp.arange(tokens_here)
    allowed = (places[None, :] < context) | (places[None, :] - context <= rows[:, None])
    score = jnp.where(allowed, score, jnp.float32(-1e30))
    top_score = jnp.max(score, axis=-1, keepdims=True)
    weight = jnp.exp(score - top_score)
    probs = (weight / jnp.sum(weight, axis=-1, keepdims=True)).astype(jnp.bfloat16)
    attended = jnp.einsum(
        "jgts,sjd->tjgd", probs, joined_values, preferred_element_type=jnp.float32
    )
    return attended.reshape(tokens_here, -1).astype(jnp.bfloat16)


def attention_kernel(q_ref, kn_ref, vn_ref, kr_ref, vr_ref, o_ref):
    tokens = q_ref.shape[0]
    group = q_ref.shape[1] // HEAD_WIDTH
    k_res = kr_ref[0]
    v_res = vr_ref[0]
    k_new = kn_ref[...]
    v_new = vn_ref[...]
    rows = lax.broadcasted_iota(jnp.int32, (tokens, tokens), 0)
    cols = lax.broadcasted_iota(jnp.int32, (tokens, tokens), 1)
    visible = cols <= rows
    scale = HEAD_WIDTH ** (-0.5)
    dims = (((1,), (1,)), ((), ()))
    for g in range(group):
        q = q_ref[:, g * HEAD_WIDTH:(g + 1) * HEAD_WIDTH]
        s_res = lax.dot_general(q, k_res, dims, preferred_element_type=jnp.float32) * scale
        s_new = lax.dot_general(q, k_new, dims, preferred_element_type=jnp.float32) * scale
        s_new = jnp.where(visible, s_new, jnp.float32(-1e30))
        top = jnp.maximum(
            jnp.max(s_res, axis=1, keepdims=True), jnp.max(s_new, axis=1, keepdims=True)
        )
        w_res = jnp.exp(s_res - top)
        w_new = jnp.exp(s_new - top)
        total = jnp.sum(w_res, axis=1, keepdims=True) + jnp.sum(w_new, axis=1, keepdims=True)
        p_res = (w_res / total).astype(jnp.bfloat16)
        p_new = (w_new / total).astype(jnp.bfloat16)
        out = jnp.dot(p_res, v_res, preferred_element_type=jnp.float32) + jnp.dot(
            p_new, v_new, preferred_element_type=jnp.float32
        )
        o_ref[:, g * HEAD_WIDTH:(g + 1) * HEAD_WIDTH] = out.astype(o_ref.dtype)


def attend_kernel(queries, fresh_keys, fresh_values, resident_keys, resident_values, interpret=False):
    tokens = queries.shape[0]
    kv_here = fresh_keys.shape[1] // HEAD_WIDTH
    width = queries.shape[1] // kv_here
    context = resident_keys.shape[1]
    return pl.pallas_call(
        attention_kernel,
        grid=(kv_here,),
        in_specs=[
            pl.BlockSpec((tokens, width), lambda j: (0, j)),
            pl.BlockSpec((tokens, HEAD_WIDTH), lambda j: (0, j)),
            pl.BlockSpec((tokens, HEAD_WIDTH), lambda j: (0, j)),
            pl.BlockSpec((1, context, HEAD_WIDTH), lambda j: (0, 0, j)),
            pl.BlockSpec((1, context, HEAD_WIDTH), lambda j: (0, 0, j)),
        ],
        out_specs=pl.BlockSpec((tokens, width), lambda j: (0, j)),
        out_shape=jax.ShapeDtypeStruct(queries.shape, jnp.bfloat16),
        interpret=interpret,
    )(queries, fresh_keys, fresh_values, resident_keys, resident_values)


def gate_up_kernel(lane_ref, mine_ref, other_ref, g_own, g_other, u_own, u_other, act_ref):
    fold = g_own.shape[0] // HEAD_WIDTH
    rows = act_ref.shape[0]
    x_mine = jnp.concatenate(
        [mine_ref[pl.ds(j, rows, stride=fold), :] for j in range(fold)], axis=1
    )
    x_other = jnp.concatenate(
        [other_ref[pl.ds(j, rows, stride=fold), :] for j in range(fold)], axis=1
    )
    gate = jnp.dot(x_mine, g_own[...], preferred_element_type=jnp.float32) + jnp.dot(
        x_other, g_other[...], preferred_element_type=jnp.float32
    )
    up = jnp.dot(x_mine, u_own[...], preferred_element_type=jnp.float32) + jnp.dot(
        x_other, u_other[...], preferred_element_type=jnp.float32
    )
    act_ref[...] = (gate / (1.0 + jnp.exp(-gate)) * up).astype(act_ref.dtype)


def down_kernel(lane_ref, act_mine, act_other, d_own, d_other, out_ref):
    fold = d_own.shape[1] // HEAD_WIDTH
    rows = act_mine.shape[0]
    out = jnp.dot(act_mine[...], d_own[...], preferred_element_type=jnp.float32) + jnp.dot(
        act_other[...], d_other[...], preferred_element_type=jnp.float32
    )
    out_ref[...] = out.astype(out_ref.dtype)


def gate_up(lane, mine, other, gate_mat, up_mat, block_rows=256, interpret=False):
    folded, lanes = mine.shape
    half, hidden = gate_mat.shape[0] // 2, gate_mat.shape[1]
    fold = half // lanes
    rows = folded // fold
    act_spec = pl.BlockSpec((block_rows * fold, lanes), lambda i, lane_ref: (i, 0))
    own_rows = pl.BlockSpec((half, hidden), lambda i, lane_ref: (lane_ref[0], 0))
    other_rows = pl.BlockSpec((half, hidden), lambda i, lane_ref: (1 - lane_ref[0], 0))
    return pl.pallas_call(
        gate_up_kernel,
        grid_spec=pltpu.PrefetchScalarGridSpec(
            num_scalar_prefetch=1,
            grid=(rows // block_rows,),
            in_specs=[act_spec, act_spec, own_rows, other_rows, own_rows, other_rows],
            out_specs=pl.BlockSpec((block_rows, hidden), lambda i, lane_ref: (i, 0)),
        ),
        out_shape=jax.ShapeDtypeStruct((rows, hidden), jnp.bfloat16),
        interpret=interpret,
    )(lane, mine, other, gate_mat, gate_mat, up_mat, up_mat)


def down(lane, act_mine, act_other, down_mat, down_other, block_rows=256, interpret=False):
    rows, hidden = act_mine.shape
    half = down_other.shape[1]
    fold = half // HEAD_WIDTH
    act_spec = pl.BlockSpec((block_rows, hidden), lambda i, lane_ref: (i, 0))
    return pl.pallas_call(
        down_kernel,
        grid_spec=pltpu.PrefetchScalarGridSpec(
            num_scalar_prefetch=1,
            grid=(rows // block_rows,),
            in_specs=[
                act_spec,
                act_spec,
                pl.BlockSpec((hidden, half), lambda i, lane_ref: (0, lane_ref[0])),
                pl.BlockSpec((hidden, half), lambda i, lane_ref: (0, 0)),
            ],
            out_specs=pl.BlockSpec((block_rows, half), lambda i, lane_ref: (i, 0)),
        ),
        out_shape=jax.ShapeDtypeStruct((rows, half), jnp.bfloat16),
        interpret=interpret,
    )(lane, act_mine, act_other, down_mat, down_other)


def swap_pair(x):
    return lax.ppermute(x, "tensor", [(0, 1), (1, 0)])


def per_device(
    queries,
    fresh_keys,
    fresh_values,
    resident_keys,
    resident_values,
    out_weight,
    residual,
    norm_gain,
    expert_ids,
    gates,
    w_gate,
    w_up,
    w_down,
):
    tokens_here = residual.shape[0]
    lane = lax.axis_index("tensor")
    half = D // lax.axis_size("tensor")
    groups = lax.axis_size("dp")
    attended = attend_kernel(queries, fresh_keys, fresh_values, resident_keys, resident_values)
    down_other = swap_pair(lax.dynamic_slice_in_dim(w_down[0], (1 - lane) * half, half, 1))
    attended, down_other = lax.optimization_barrier((attended, down_other))

    here = lax.axis_index("dp")
    blocks = [jnp.dot(attended, out_weight, preferred_element_type=jnp.float32)]
    for shift in range(1, groups):
        onward = [(i, (i + shift) % groups) for i in range(groups)]
        backward = [(i, (i - shift) % groups) for i in range(groups)]
        arrived = lax.ppermute(attended, "dp", onward)
        product = jnp.dot(arrived, out_weight, preferred_element_type=jnp.float32)
        blocks.append(lax.ppermute(product, "dp", backward))
    stacked = jnp.stack(blocks)
    order = (jnp.arange(groups) - here) % groups
    mine = stacked[order].transpose(1, 0, 2).reshape(tokens_here, D)
    summed = mine + swap_pair(mine)
    hidden = residual.astype(jnp.float32) + summed
    mean_square = jnp.mean(hidden * hidden, axis=-1, keepdims=True)
    normed = (hidden * lax.rsqrt(mean_square + 1e-06) * norm_gain).astype(jnp.bfloat16)
    hidden_half = lax.dynamic_slice_in_dim(hidden, lane * half, half, 1)
    normed_half = lax.dynamic_slice_in_dim(normed, lane * half, half, 1)

    owners = lax.axis_size("dp") * lax.axis_size("expert")
    onehot = (expert_ids[:, :, None] == jnp.arange(owners)[None, None, :]).astype(jnp.int32)
    per_token = jnp.sum(onehot, axis=1)
    before = jnp.cumsum(per_token, axis=0) - per_token
    slot = jnp.sum(onehot * before[:, None, :], axis=-1)
    code = expert_ids * CAP + slot
    pick = (code[:, :, None] == jnp.arange(owners * CAP)[None, None, :]).astype(jnp.bfloat16)
    spread = jnp.sum(pick, axis=1)
    lanes = 128
    width = half // lanes
    outgoing = jnp.einsum(
        "tr,tjl->rjl", spread, normed_half.reshape(tokens_here, width, lanes),
        preferred_element_type=jnp.float32,
    ).astype(jnp.bfloat16)
    received = lax.all_to_all(
        outgoing.reshape(owners, CAP * width, lanes), ("dp", "expert"), split_axis=0, concat_axis=0, tiled=True
    ).reshape(owners * CAP * width, lanes)
    other = swap_pair(received)
    lane_id = lane.astype(jnp.int32).reshape(1)
    act = gate_up(lane_id, received, other, w_gate[0], w_up[0])
    expert_out = down(lane_id, act, swap_pair(act), w_down[0], down_other)

    returned = lax.all_to_all(
        expert_out.reshape(owners, CAP * width, lanes), ("dp", "expert"), split_axis=0, concat_axis=0, tiled=True
    ).reshape(owners * CAP, width, lanes)
    picked = jnp.einsum("tkr,rjl->tkjl", pick, returned, preferred_element_type=jnp.float32)
    moe = jnp.sum(gates[:, :, None, None] * picked, axis=1).reshape(tokens_here, half)
    return (hidden_half + moe).astype(jnp.bfloat16)


def solution(mesh):
    return jax.shard_map(
        per_device,
        mesh=mesh,
        in_specs=(
            P(("dp", "expert"), "tensor"),
            P(("dp", "expert"), "tensor"),
            P(("dp", "expert"), "tensor"),
            P(("dp", "expert"), None, "tensor"),
            P(("dp", "expert"), None, "tensor"),
            P("tensor", "dp"),
            P(("dp", "expert"), None),
            P(),
            P(("dp", "expert"), None),
            P(("dp", "expert"), None),
            P(("dp", "expert"), None, "tensor"),
            P(("dp", "expert"), None, "tensor"),
            P(("dp", "expert"), "tensor", None),
        ),
        out_specs=P(("dp", "expert"), "tensor"),
        check_vma=False,
    )
```

```python
import jax
import jax.numpy as jnp
from jax import lax
from jax.experimental import pallas as pl
from jax.experimental.pallas import tpu as pltpu
from jax.sharding import PartitionSpec as P

D = 2048
HEAD_WIDTH = 128
CAP = 6


def attend_local(queries, fresh_keys, fresh_values, resident_keys, resident_values):
    tokens_here = queries.shape[0]
    kv_here = fresh_keys.shape[1] // HEAD_WIDTH
    query_group = queries.shape[1] // HEAD_WIDTH // kv_here
    context = resident_keys.shape[1]
    query_rows = queries.reshape(tokens_here, kv_here, query_group, HEAD_WIDTH)
    joined_keys = jnp.concatenate([resident_keys[0], fresh_keys], 0).reshape(
        context + tokens_here, kv_here, HEAD_WIDTH
    )
    joined_values = jnp.concatenate([resident_values[0], fresh_values], 0).reshape(
        context + tokens_here, kv_here, HEAD_WIDTH
    )
    score = jnp.einsum(
        "tjgd,sjd->jgts", query_rows, joined_keys, preferred_element_type=jnp.float32
    ) * HEAD_WIDTH ** (-0.5)
    places = jnp.arange(context + tokens_here)
    rows = jnp.arange(tokens_here)
    allowed = (places[None, :] < context) | (places[None, :] - context <= rows[:, None])
    score = jnp.where(allowed, score, jnp.float32(-1e30))
    top_score = jnp.max(score, axis=-1, keepdims=True)
    weight = jnp.exp(score - top_score)
    probs = (weight / jnp.sum(weight, axis=-1, keepdims=True)).astype(jnp.bfloat16)
    attended = jnp.einsum(
        "jgts,sjd->tjgd", probs, joined_values, preferred_element_type=jnp.float32
    )
    return attended.reshape(tokens_here, -1).astype(jnp.bfloat16)


def attention_kernel(q_ref, kn_ref, vn_ref, kr_ref, vr_ref, o_ref):
    tokens = q_ref.shape[0]
    group = q_ref.shape[1] // HEAD_WIDTH
    k_res = kr_ref[0]
    v_res = vr_ref[0]
    k_new = kn_ref[...]
    v_new = vn_ref[...]
    q = jnp.concatenate(
        [q_ref[:, g * HEAD_WIDTH:(g + 1) * HEAD_WIDTH] for g in range(group)], axis=0
    )
    rows = lax.broadcasted_iota(jnp.int32, (group * tokens, tokens), 0) % tokens
    cols = lax.broadcasted_iota(jnp.int32, (group * tokens, tokens), 1)
    visible = cols <= rows
    scale = HEAD_WIDTH ** (-0.5)
    dims = (((1,), (1,)), ((), ()))
    s_res = lax.dot_general(q, k_res, dims, preferred_element_type=jnp.float32) * scale
    s_new = lax.dot_general(q, k_new, dims, preferred_element_type=jnp.float32) * scale
    s_new = jnp.where(visible, s_new, jnp.float32(-1e30))
    top = jnp.maximum(
        jnp.max(s_res, axis=1, keepdims=True), jnp.max(s_new, axis=1, keepdims=True)
    )
    w_res = jnp.exp(s_res - top)
    w_new = jnp.exp(s_new - top)
    total = jnp.sum(w_res, axis=1, keepdims=True) + jnp.sum(w_new, axis=1, keepdims=True)
    p_res = (w_res / total).astype(jnp.bfloat16)
    p_new = (w_new / total).astype(jnp.bfloat16)
    out = jnp.dot(p_res, v_res, preferred_element_type=jnp.float32) + jnp.dot(
        p_new, v_new, preferred_element_type=jnp.float32
    )
    out = out.astype(o_ref.dtype)
    for g in range(group):
        o_ref[:, g * HEAD_WIDTH:(g + 1) * HEAD_WIDTH] = out[g * tokens:(g + 1) * tokens]


def attend_kernel(queries, fresh_keys, fresh_values, resident_keys, resident_values, interpret=False):
    tokens = queries.shape[0]
    kv_here = fresh_keys.shape[1] // HEAD_WIDTH
    width = queries.shape[1] // kv_here
    context = resident_keys.shape[1]
    return pl.pallas_call(
        attention_kernel,
        grid=(kv_here,),
        in_specs=[
            pl.BlockSpec((tokens, width), lambda j: (0, j)),
            pl.BlockSpec((tokens, HEAD_WIDTH), lambda j: (0, j)),
            pl.BlockSpec((tokens, HEAD_WIDTH), lambda j: (0, j)),
            pl.BlockSpec((1, context, HEAD_WIDTH), lambda j: (0, 0, j)),
            pl.BlockSpec((1, context, HEAD_WIDTH), lambda j: (0, 0, j)),
        ],
        out_specs=pl.BlockSpec((tokens, width), lambda j: (0, j)),
        out_shape=jax.ShapeDtypeStruct(queries.shape, jnp.bfloat16),
        interpret=interpret,
    )(queries, fresh_keys, fresh_values, resident_keys, resident_values)


def gate_up_kernel(lane_ref, mine_ref, other_ref, g_own, g_other, u_own, u_other, act_ref):
    fold = g_own.shape[0] // HEAD_WIDTH
    rows = act_ref.shape[0]
    x_mine = jnp.concatenate(
        [mine_ref[pl.ds(j, rows, stride=fold), :] for j in range(fold)], axis=1
    )
    x_other = jnp.concatenate(
        [other_ref[pl.ds(j, rows, stride=fold), :] for j in range(fold)], axis=1
    )
    gate = jnp.dot(x_mine, g_own[...], preferred_element_type=jnp.float32) + jnp.dot(
        x_other, g_other[...], preferred_element_type=jnp.float32
    )
    up = jnp.dot(x_mine, u_own[...], preferred_element_type=jnp.float32) + jnp.dot(
        x_other, u_other[...], preferred_element_type=jnp.float32
    )
    act_ref[...] = (gate / (1.0 + jnp.exp(-gate)) * up).astype(act_ref.dtype)


def down_kernel(lane_ref, act_mine, act_other, d_own, d_other, out_ref):
    fold = d_own.shape[1] // HEAD_WIDTH
    rows = act_mine.shape[0]
    out = jnp.dot(act_mine[...], d_own[...], preferred_element_type=jnp.float32) + jnp.dot(
        act_other[...], d_other[...], preferred_element_type=jnp.float32
    )
    for j in range(fold):
        out_ref[pl.ds(j, rows, stride=fold), :] = out[:, j * HEAD_WIDTH:(j + 1) * HEAD_WIDTH]


def gate_up(lane, mine, other, gate_mat, up_mat, block_rows=256, interpret=False):
    folded, lanes = mine.shape
    half, hidden = gate_mat.shape[0] // 2, gate_mat.shape[1]
    fold = half // lanes
    rows = folded // fold
    act_spec = pl.BlockSpec((block_rows * fold, lanes), lambda i, lane_ref: (i, 0))
    own_rows = pl.BlockSpec((half, hidden), lambda i, lane_ref: (lane_ref[0], 0))
    other_rows = pl.BlockSpec((half, hidden), lambda i, lane_ref: (1 - lane_ref[0], 0))
    return pl.pallas_call(
        gate_up_kernel,
        grid_spec=pltpu.PrefetchScalarGridSpec(
            num_scalar_prefetch=1,
            grid=(rows // block_rows,),
            in_specs=[act_spec, act_spec, own_rows, other_rows, own_rows, other_rows],
            out_specs=pl.BlockSpec((block_rows, hidden), lambda i, lane_ref: (i, 0)),
        ),
        out_shape=jax.ShapeDtypeStruct((rows, hidden), jnp.bfloat16),
        interpret=interpret,
    )(lane, mine, other, gate_mat, gate_mat, up_mat, up_mat)


def down(lane, act_mine, act_other, down_mat, down_other, block_rows=256, interpret=False):
    rows, hidden = act_mine.shape
    half = down_other.shape[1]
    fold = half // HEAD_WIDTH
    act_spec = pl.BlockSpec((block_rows, hidden), lambda i, lane_ref: (i, 0))
    return pl.pallas_call(
        down_kernel,
        grid_spec=pltpu.PrefetchScalarGridSpec(
            num_scalar_prefetch=1,
            grid=(rows // block_rows,),
            in_specs=[
                act_spec,
                act_spec,
                pl.BlockSpec((hidden, half), lambda i, lane_ref: (0, lane_ref[0])),
                pl.BlockSpec((hidden, half), lambda i, lane_ref: (0, 0)),
            ],
            out_specs=pl.BlockSpec((block_rows * fold, HEAD_WIDTH), lambda i, lane_ref: (i, 0)),
        ),
        out_shape=jax.ShapeDtypeStruct((rows * fold, HEAD_WIDTH), jnp.float32),
        interpret=interpret,
    )(lane, act_mine, act_other, down_mat, down_other)


def swap_pair(x):
    return lax.ppermute(x, "tensor", [(0, 1), (1, 0)])


def per_device(
    queries,
    fresh_keys,
    fresh_values,
    resident_keys,
    resident_values,
    out_weight,
    residual,
    norm_gain,
    expert_ids,
    gates,
    w_gate,
    w_up,
    w_down,
):
    tokens_here = residual.shape[0]
    lane = lax.axis_index("tensor")
    half = D // lax.axis_size("tensor")
    groups = lax.axis_size("dp")
    attended = attend_kernel(queries, fresh_keys, fresh_values, resident_keys, resident_values)

    here = lax.axis_index("dp")
    blocks = [jnp.dot(attended, out_weight, preferred_element_type=jnp.float32)]
    for shift in range(1, groups):
        onward = [(i, (i + shift) % groups) for i in range(groups)]
        backward = [(i, (i - shift) % groups) for i in range(groups)]
        arrived = lax.ppermute(attended, "dp", onward)
        product = jnp.dot(arrived, out_weight, preferred_element_type=jnp.float32)
        blocks.append(lax.ppermute(product, "dp", backward))
    stacked = jnp.stack(blocks)
    order = (jnp.arange(groups) - here) % groups
    mine = stacked[order].transpose(1, 0, 2).reshape(tokens_here, D)
    summed = mine + swap_pair(mine)
    hidden = residual.astype(jnp.float32) + summed
    mean_square = jnp.mean(hidden * hidden, axis=-1, keepdims=True)
    normed = (hidden * lax.rsqrt(mean_square + 1e-06) * norm_gain).astype(jnp.bfloat16)
    hidden_half = lax.dynamic_slice_in_dim(hidden, lane * half, half, 1)
    normed_half = lax.dynamic_slice_in_dim(normed, lane * half, half, 1)

    owners = lax.axis_size("dp") * lax.axis_size("expert")
    onehot = (expert_ids[:, :, None] == jnp.arange(owners)[None, None, :]).astype(jnp.int32)
    per_token = jnp.sum(onehot, axis=1)
    before = jnp.cumsum(per_token, axis=0) - per_token
    slot = jnp.sum(onehot * before[:, None, :], axis=-1)
    code = expert_ids * CAP + slot
    pick = (code[:, :, None] == jnp.arange(owners * CAP)[None, None, :]).astype(jnp.bfloat16)
    spread = jnp.sum(pick, axis=1)
    lanes = 128
    width = half // lanes
    outgoing = jnp.einsum(
        "tr,tjl->rjl", spread, normed_half.reshape(tokens_here, width, lanes),
        preferred_element_type=jnp.float32,
    ).astype(jnp.bfloat16)
    received = lax.all_to_all(
        outgoing.reshape(owners, CAP * width, lanes), ("dp", "expert"), split_axis=0, concat_axis=0, tiled=True
    ).reshape(owners * CAP * width, lanes)
    other = swap_pair(received)
    lane_id = lane.astype(jnp.int32).reshape(1)
    down_other = swap_pair(lax.dynamic_slice_in_dim(w_down[0], (1 - lane) * half, half, 1))
    act = gate_up(lane_id, received, other, w_gate[0], w_up[0])
    expert_out = down(lane_id, act, swap_pair(act), w_down[0], down_other).astype(jnp.bfloat16)

    returned = lax.all_to_all(
        expert_out.reshape(owners, CAP * width, lanes), ("dp", "expert"), split_axis=0, concat_axis=0, tiled=True
    ).reshape(owners * CAP, width, lanes)
    picked = jnp.einsum("tkr,rjl->tkjl", pick, returned, preferred_element_type=jnp.float32)
    moe = jnp.sum(gates[:, :, None, None] * picked, axis=1).reshape(tokens_here, half)
    return (hidden_half + moe).astype(jnp.bfloat16)


def solution(mesh):
    return jax.shard_map(
        per_device,
        mesh=mesh,
        in_specs=(
            P(("dp", "expert"), "tensor"),
            P(("dp", "expert"), "tensor"),
            P(("dp", "expert"), "tensor"),
            P(("dp", "expert"), None, "tensor"),
            P(("dp", "expert"), None, "tensor"),
            P("tensor", "dp"),
            P(("dp", "expert"), None),
            P(),
            P(("dp", "expert"), None),
            P(("dp", "expert"), None),
            P(("dp", "expert"), None, "tensor"),
            P(("dp", "expert"), None, "tensor"),
            P(("dp", "expert"), "tensor", None),
        ),
        out_specs=P(("dp", "expert"), "tensor"),
        check_vma=False,
    )
```

```python
import jax
import jax.numpy as jnp
from jax import lax
from jax.experimental import pallas as pl
from jax.experimental.pallas import tpu as pltpu
from jax.sharding import PartitionSpec as P

D = 2048
HEAD_WIDTH = 128
CAP = 6


def attend_local(queries, fresh_keys, fresh_values, resident_keys, resident_values):
    tokens_here = queries.shape[0]
    kv_here = fresh_keys.shape[1] // HEAD_WIDTH
    query_group = queries.shape[1] // HEAD_WIDTH // kv_here
    context = resident_keys.shape[1]
    query_rows = queries.reshape(tokens_here, kv_here, query_group, HEAD_WIDTH)
    joined_keys = jnp.concatenate([resident_keys[0], fresh_keys], 0).reshape(
        context + tokens_here, kv_here, HEAD_WIDTH
    )
    joined_values = jnp.concatenate([resident_values[0], fresh_values], 0).reshape(
        context + tokens_here, kv_here, HEAD_WIDTH
    )
    score = jnp.einsum(
        "tjgd,sjd->jgts", query_rows, joined_keys, preferred_element_type=jnp.float32
    ) * HEAD_WIDTH ** (-0.5)
    places = jnp.arange(context + tokens_here)
    rows = jnp.arange(tokens_here)
    allowed = (places[None, :] < context) | (places[None, :] - context <= rows[:, None])
    score = jnp.where(allowed, score, jnp.float32(-1e30))
    top_score = jnp.max(score, axis=-1, keepdims=True)
    weight = jnp.exp(score - top_score)
    probs = (weight / jnp.sum(weight, axis=-1, keepdims=True)).astype(jnp.bfloat16)
    attended = jnp.einsum(
        "jgts,sjd->tjgd", probs, joined_values, preferred_element_type=jnp.float32
    )
    return attended.reshape(tokens_here, -1).astype(jnp.bfloat16)


def attention_kernel(q_ref, kn_ref, vn_ref, kr_ref, vr_ref, o_ref):
    tokens = q_ref.shape[0]
    group = q_ref.shape[1] // HEAD_WIDTH
    k_res = kr_ref[0]
    v_res = vr_ref[0]
    k_new = kn_ref[...]
    v_new = vn_ref[...]
    q = jnp.concatenate(
        [q_ref[:, g * HEAD_WIDTH:(g + 1) * HEAD_WIDTH] for g in range(group)], axis=0
    )
    rows = lax.broadcasted_iota(jnp.int32, (group * tokens, tokens), 0) % tokens
    cols = lax.broadcasted_iota(jnp.int32, (group * tokens, tokens), 1)
    visible = cols <= rows
    scale = HEAD_WIDTH ** (-0.5)
    dims = (((1,), (1,)), ((), ()))
    s_res = lax.dot_general(q, k_res, dims, preferred_element_type=jnp.float32) * scale
    s_new = lax.dot_general(q, k_new, dims, preferred_element_type=jnp.float32) * scale
    s_new = jnp.where(visible, s_new, jnp.float32(-1e30))
    top = jnp.maximum(
        jnp.max(s_res, axis=1, keepdims=True), jnp.max(s_new, axis=1, keepdims=True)
    )
    w_res = jnp.exp(s_res - top)
    w_new = jnp.exp(s_new - top)
    total = jnp.sum(w_res, axis=1, keepdims=True) + jnp.sum(w_new, axis=1, keepdims=True)
    p_res = (w_res / total).astype(jnp.bfloat16)
    p_new = (w_new / total).astype(jnp.bfloat16)
    out = jnp.dot(p_res, v_res, preferred_element_type=jnp.float32) + jnp.dot(
        p_new, v_new, preferred_element_type=jnp.float32
    )
    out = out.astype(o_ref.dtype)
    for g in range(group):
        o_ref[:, g * HEAD_WIDTH:(g + 1) * HEAD_WIDTH] = out[g * tokens:(g + 1) * tokens]


def attend_kernel(queries, fresh_keys, fresh_values, resident_keys, resident_values, interpret=False):
    tokens = queries.shape[0]
    kv_here = fresh_keys.shape[1] // HEAD_WIDTH
    width = queries.shape[1] // kv_here
    context = resident_keys.shape[1]
    return pl.pallas_call(
        attention_kernel,
        grid=(kv_here,),
        in_specs=[
            pl.BlockSpec((tokens, width), lambda j: (0, j)),
            pl.BlockSpec((tokens, HEAD_WIDTH), lambda j: (0, j)),
            pl.BlockSpec((tokens, HEAD_WIDTH), lambda j: (0, j)),
            pl.BlockSpec((1, context, HEAD_WIDTH), lambda j: (0, 0, j)),
            pl.BlockSpec((1, context, HEAD_WIDTH), lambda j: (0, 0, j)),
        ],
        out_specs=pl.BlockSpec((tokens, width), lambda j: (0, j)),
        out_shape=jax.ShapeDtypeStruct(queries.shape, jnp.bfloat16),
        interpret=interpret,
    )(queries, fresh_keys, fresh_values, resident_keys, resident_values)


def gate_up_kernel(lane_ref, mine_ref, other_ref, g_own, g_other, u_own, u_other, act_ref):
    fold = g_own.shape[0] // HEAD_WIDTH
    rows = act_ref.shape[0]
    x_mine = jnp.concatenate(
        [mine_ref[pl.ds(j, rows, stride=fold), :] for j in range(fold)], axis=1
    )
    x_other = jnp.concatenate(
        [other_ref[pl.ds(j, rows, stride=fold), :] for j in range(fold)], axis=1
    )
    gate = jnp.dot(x_mine, g_own[...], preferred_element_type=jnp.float32) + jnp.dot(
        x_other, g_other[...], preferred_element_type=jnp.float32
    )
    up = jnp.dot(x_mine, u_own[...], preferred_element_type=jnp.float32) + jnp.dot(
        x_other, u_other[...], preferred_element_type=jnp.float32
    )
    act_ref[...] = (gate / (1.0 + jnp.exp(-gate)) * up).astype(act_ref.dtype)


def down_kernel(lane_ref, act_mine, act_other, d_own, d_other, out_ref, fold_ref):
    fold = d_own.shape[1] // HEAD_WIDTH
    rows = act_mine.shape[0]
    out = jnp.dot(act_mine[...], d_own[...], preferred_element_type=jnp.float32) + jnp.dot(
        act_other[...], d_other[...], preferred_element_type=jnp.float32
    )
    for j in range(fold):
        fold_ref[pl.ds(j, rows, stride=fold), :] = out[:, j * HEAD_WIDTH:(j + 1) * HEAD_WIDTH]
    out_ref[...] = fold_ref[...].astype(out_ref.dtype)


def gate_up(lane, mine, other, gate_mat, up_mat, block_rows=256, interpret=False):
    folded, lanes = mine.shape
    half, hidden = gate_mat.shape[0] // 2, gate_mat.shape[1]
    fold = half // lanes
    rows = folded // fold
    act_spec = pl.BlockSpec((block_rows * fold, lanes), lambda i, lane_ref: (i, 0))
    own_rows = pl.BlockSpec((half, hidden), lambda i, lane_ref: (lane_ref[0], 0))
    other_rows = pl.BlockSpec((half, hidden), lambda i, lane_ref: (1 - lane_ref[0], 0))
    return pl.pallas_call(
        gate_up_kernel,
        grid_spec=pltpu.PrefetchScalarGridSpec(
            num_scalar_prefetch=1,
            grid=(rows // block_rows,),
            in_specs=[act_spec, act_spec, own_rows, other_rows, own_rows, other_rows],
            out_specs=pl.BlockSpec((block_rows, hidden), lambda i, lane_ref: (i, 0)),
        ),
        out_shape=jax.ShapeDtypeStruct((rows, hidden), jnp.bfloat16),
        interpret=interpret,
    )(lane, mine, other, gate_mat, gate_mat, up_mat, up_mat)


def down(lane, act_mine, act_other, down_mat, down_other, block_rows=256, interpret=False):
    rows, hidden = act_mine.shape
    half = down_other.shape[1]
    fold = half // HEAD_WIDTH
    act_spec = pl.BlockSpec((block_rows, hidden), lambda i, lane_ref: (i, 0))
    return pl.pallas_call(
        down_kernel,
        grid_spec=pltpu.PrefetchScalarGridSpec(
            num_scalar_prefetch=1,
            grid=(rows // block_rows,),
            in_specs=[
                act_spec,
                act_spec,
                pl.BlockSpec((hidden, half), lambda i, lane_ref: (0, lane_ref[0])),
                pl.BlockSpec((hidden, half), lambda i, lane_ref: (0, 0)),
            ],
            out_specs=pl.BlockSpec((block_rows * fold, HEAD_WIDTH), lambda i, lane_ref: (i, 0)),
            scratch_shapes=[pltpu.VMEM((block_rows * fold, HEAD_WIDTH), jnp.float32)],
        ),
        out_shape=jax.ShapeDtypeStruct((rows * fold, HEAD_WIDTH), jnp.bfloat16),
        interpret=interpret,
    )(lane, act_mine, act_other, down_mat, down_other)


def swap_pair(x):
    return lax.ppermute(x, "tensor", [(0, 1), (1, 0)])


def per_device(
    queries,
    fresh_keys,
    fresh_values,
    resident_keys,
    resident_values,
    out_weight,
    residual,
    norm_gain,
    expert_ids,
    gates,
    w_gate,
    w_up,
    w_down,
):
    tokens_here = residual.shape[0]
    lane = lax.axis_index("tensor")
    half = D // lax.axis_size("tensor")
    groups = lax.axis_size("dp")
    attended = attend_kernel(queries, fresh_keys, fresh_values, resident_keys, resident_values)

    here = lax.axis_index("dp")
    blocks = [jnp.dot(attended, out_weight, preferred_element_type=jnp.float32)]
    for shift in range(1, groups):
        onward = [(i, (i + shift) % groups) for i in range(groups)]
        backward = [(i, (i - shift) % groups) for i in range(groups)]
        arrived = lax.ppermute(attended, "dp", onward)
        product = jnp.dot(arrived, out_weight, preferred_element_type=jnp.float32)
        blocks.append(lax.ppermute(product, "dp", backward))
    stacked = jnp.stack(blocks)
    order = (jnp.arange(groups) - here) % groups
    mine = stacked[order].transpose(1, 0, 2).reshape(tokens_here, D)
    summed = mine + swap_pair(mine)
    hidden = residual.astype(jnp.float32) + summed
    mean_square = jnp.mean(hidden * hidden, axis=-1, keepdims=True)
    normed = (hidden * lax.rsqrt(mean_square + 1e-06) * norm_gain).astype(jnp.bfloat16)
    hidden_half = lax.dynamic_slice_in_dim(hidden, lane * half, half, 1)
    normed_half = lax.dynamic_slice_in_dim(normed, lane * half, half, 1)

    owners = lax.axis_size("dp") * lax.axis_size("expert")
    onehot = (expert_ids[:, :, None] == jnp.arange(owners)[None, None, :]).astype(jnp.int32)
    per_token = jnp.sum(onehot, axis=1)
    before = jnp.cumsum(per_token, axis=0) - per_token
    slot = jnp.sum(onehot * before[:, None, :], axis=-1)
    code = expert_ids * CAP + slot
    pick = (code[:, :, None] == jnp.arange(owners * CAP)[None, None, :]).astype(jnp.bfloat16)
    spread = jnp.sum(pick, axis=1)
    lanes = 128
    width = half // lanes
    outgoing = jnp.einsum(
        "tr,tjl->rjl", spread, normed_half.reshape(tokens_here, width, lanes),
        preferred_element_type=jnp.float32,
    ).astype(jnp.bfloat16)
    received = lax.all_to_all(
        outgoing.reshape(owners, CAP * width, lanes), ("dp", "expert"), split_axis=0, concat_axis=0, tiled=True
    ).reshape(owners * CAP * width, lanes)
    other = swap_pair(received)
    lane_id = lane.astype(jnp.int32).reshape(1)
    down_other = swap_pair(lax.dynamic_slice_in_dim(w_down[0], (1 - lane) * half, half, 1))
    act = gate_up(lane_id, received, other, w_gate[0], w_up[0])
    expert_out = down(lane_id, act, swap_pair(act), w_down[0], down_other)

    returned = lax.all_to_all(
        expert_out.reshape(owners, CAP * width, lanes), ("dp", "expert"), split_axis=0, concat_axis=0, tiled=True
    ).reshape(owners * CAP, width, lanes)
    picked = jnp.einsum("tkr,rjl->tkjl", pick, returned, preferred_element_type=jnp.float32)
    moe = jnp.sum(gates[:, :, None, None] * picked, axis=1).reshape(tokens_here, half)
    return (hidden_half + moe).astype(jnp.bfloat16)


def solution(mesh):
    return jax.shard_map(
        per_device,
        mesh=mesh,
        in_specs=(
            P(("dp", "expert"), "tensor"),
            P(("dp", "expert"), "tensor"),
            P(("dp", "expert"), "tensor"),
            P(("dp", "expert"), None, "tensor"),
            P(("dp", "expert"), None, "tensor"),
            P("tensor", "dp"),
            P(("dp", "expert"), None),
            P(),
            P(("dp", "expert"), None),
            P(("dp", "expert"), None),
            P(("dp", "expert"), None, "tensor"),
            P(("dp", "expert"), None, "tensor"),
            P(("dp", "expert"), "tensor", None),
        ),
        out_specs=P(("dp", "expert"), "tensor"),
        check_vma=False,
    )
```

```python
import jax
import jax.numpy as jnp
from jax import lax
from jax.experimental import pallas as pl
from jax.experimental.pallas import tpu as pltpu
from jax.sharding import PartitionSpec as P

D = 2048
HEAD_WIDTH = 128
CAP = 6


def attend_local(queries, fresh_keys, fresh_values, resident_keys, resident_values):
    tokens_here = queries.shape[0]
    kv_here = fresh_keys.shape[1] // HEAD_WIDTH
    query_group = queries.shape[1] // HEAD_WIDTH // kv_here
    context = resident_keys.shape[1]
    query_rows = queries.reshape(tokens_here, kv_here, query_group, HEAD_WIDTH)
    joined_keys = jnp.concatenate([resident_keys[0], fresh_keys], 0).reshape(
        context + tokens_here, kv_here, HEAD_WIDTH
    )
    joined_values = jnp.concatenate([resident_values[0], fresh_values], 0).reshape(
        context + tokens_here, kv_here, HEAD_WIDTH
    )
    score = jnp.einsum(
        "tjgd,sjd->jgts", query_rows, joined_keys, preferred_element_type=jnp.float32
    ) * HEAD_WIDTH ** (-0.5)
    places = jnp.arange(context + tokens_here)
    rows = jnp.arange(tokens_here)
    allowed = (places[None, :] < context) | (places[None, :] - context <= rows[:, None])
    score = jnp.where(allowed, score, jnp.float32(-1e30))
    top_score = jnp.max(score, axis=-1, keepdims=True)
    weight = jnp.exp(score - top_score)
    probs = (weight / jnp.sum(weight, axis=-1, keepdims=True)).astype(jnp.bfloat16)
    attended = jnp.einsum(
        "jgts,sjd->tjgd", probs, joined_values, preferred_element_type=jnp.float32
    )
    return attended.reshape(tokens_here, -1).astype(jnp.bfloat16)


def attention_kernel(q_ref, kn_ref, vn_ref, kr_ref, vr_ref, o_ref):
    tokens = q_ref.shape[0]
    group = q_ref.shape[1] // HEAD_WIDTH
    k_res = kr_ref[0]
    v_res = vr_ref[0]
    k_new = kn_ref[...]
    v_new = vn_ref[...]
    q = jnp.concatenate(
        [q_ref[:, g * HEAD_WIDTH:(g + 1) * HEAD_WIDTH] for g in range(group)], axis=0
    )
    rows = lax.broadcasted_iota(jnp.int32, (group * tokens, tokens), 0) % tokens
    cols = lax.broadcasted_iota(jnp.int32, (group * tokens, tokens), 1)
    visible = cols <= rows
    scale = HEAD_WIDTH ** (-0.5)
    dims = (((1,), (1,)), ((), ()))
    s_res = lax.dot_general(q, k_res, dims, preferred_element_type=jnp.float32) * scale
    s_new = lax.dot_general(q, k_new, dims, preferred_element_type=jnp.float32) * scale
    s_new = jnp.where(visible, s_new, jnp.float32(-1e30))
    top = jnp.maximum(
        jnp.max(s_res, axis=1, keepdims=True), jnp.max(s_new, axis=1, keepdims=True)
    )
    w_res = jnp.exp(s_res - top)
    w_new = jnp.exp(s_new - top)
    total = jnp.sum(w_res, axis=1, keepdims=True) + jnp.sum(w_new, axis=1, keepdims=True)
    p_res = (w_res / total).astype(jnp.bfloat16)
    p_new = (w_new / total).astype(jnp.bfloat16)
    out = jnp.dot(p_res, v_res, preferred_element_type=jnp.float32) + jnp.dot(
        p_new, v_new, preferred_element_type=jnp.float32
    )
    out = out.astype(o_ref.dtype)
    for g in range(group):
        o_ref[:, g * HEAD_WIDTH:(g + 1) * HEAD_WIDTH] = out[g * tokens:(g + 1) * tokens]


def attend_kernel(queries, fresh_keys, fresh_values, resident_keys, resident_values, interpret=False):
    tokens = queries.shape[0]
    kv_here = fresh_keys.shape[1] // HEAD_WIDTH
    width = queries.shape[1] // kv_here
    context = resident_keys.shape[1]
    return pl.pallas_call(
        attention_kernel,
        grid=(kv_here,),
        in_specs=[
            pl.BlockSpec((tokens, width), lambda j: (0, j)),
            pl.BlockSpec((tokens, HEAD_WIDTH), lambda j: (0, j)),
            pl.BlockSpec((tokens, HEAD_WIDTH), lambda j: (0, j)),
            pl.BlockSpec((1, context, HEAD_WIDTH), lambda j: (0, 0, j)),
            pl.BlockSpec((1, context, HEAD_WIDTH), lambda j: (0, 0, j)),
        ],
        out_specs=pl.BlockSpec((tokens, width), lambda j: (0, j)),
        out_shape=jax.ShapeDtypeStruct(queries.shape, jnp.bfloat16),
        interpret=interpret,
    )(queries, fresh_keys, fresh_values, resident_keys, resident_values)


def gate_up_kernel(lane_ref, mine_ref, other_ref, g_own, g_other, u_own, u_other, act_ref):
    fold = g_own.shape[0] // HEAD_WIDTH
    rows = act_ref.shape[0]
    x_mine = jnp.concatenate(
        [mine_ref[pl.ds(j, rows, stride=fold), :] for j in range(fold)], axis=1
    )
    x_other = jnp.concatenate(
        [other_ref[pl.ds(j, rows, stride=fold), :] for j in range(fold)], axis=1
    )
    gate = jnp.dot(x_mine, g_own[...], preferred_element_type=jnp.float32) + jnp.dot(
        x_other, g_other[...], preferred_element_type=jnp.float32
    )
    up = jnp.dot(x_mine, u_own[...], preferred_element_type=jnp.float32) + jnp.dot(
        x_other, u_other[...], preferred_element_type=jnp.float32
    )
    act_ref[...] = (gate / (1.0 + jnp.exp(-gate)) * up).astype(act_ref.dtype)


def down_kernel(lane_ref, act_mine, act_other, d_own, d_other, out_ref, fold_ref):
    fold = d_own.shape[1] // HEAD_WIDTH
    rows = act_mine.shape[0]
    out = jnp.dot(act_mine[...], d_own[...], preferred_element_type=jnp.float32) + jnp.dot(
        act_other[...], d_other[...], preferred_element_type=jnp.float32
    )
    for j in range(fold):
        fold_ref[pl.ds(j, rows, stride=fold), :] = out[:, j * HEAD_WIDTH:(j + 1) * HEAD_WIDTH]
    out_ref[...] = fold_ref[...].astype(out_ref.dtype)


def gate_up(lane, mine, other, gate_mat, up_mat, block_rows=256, interpret=False):
    folded, lanes = mine.shape
    half, hidden = gate_mat.shape[0] // 2, gate_mat.shape[1]
    fold = half // lanes
    rows = folded // fold
    act_spec = pl.BlockSpec((block_rows * fold, lanes), lambda i, lane_ref: (i, 0))
    own_rows = pl.BlockSpec((half, hidden), lambda i, lane_ref: (lane_ref[0], 0))
    other_rows = pl.BlockSpec((half, hidden), lambda i, lane_ref: (1 - lane_ref[0], 0))
    return pl.pallas_call(
        gate_up_kernel,
        grid_spec=pltpu.PrefetchScalarGridSpec(
            num_scalar_prefetch=1,
            grid=(rows // block_rows,),
            in_specs=[act_spec, act_spec, own_rows, other_rows, own_rows, other_rows],
            out_specs=pl.BlockSpec((block_rows, hidden), lambda i, lane_ref: (i, 0)),
        ),
        out_shape=jax.ShapeDtypeStruct((rows, hidden), jnp.bfloat16),
        interpret=interpret,
    )(lane, mine, other, gate_mat, gate_mat, up_mat, up_mat)


def down(lane, act_mine, act_other, down_mat, down_other, block_rows=256, interpret=False):
    rows, hidden = act_mine.shape
    half = down_other.shape[1] // 2
    fold = half // HEAD_WIDTH
    act_spec = pl.BlockSpec((block_rows, hidden), lambda i, lane_ref: (i, 0))
    return pl.pallas_call(
        down_kernel,
        grid_spec=pltpu.PrefetchScalarGridSpec(
            num_scalar_prefetch=1,
            grid=(rows // block_rows,),
            in_specs=[
                act_spec,
                act_spec,
                pl.BlockSpec((hidden, half), lambda i, lane_ref: (0, lane_ref[0])),
                pl.BlockSpec((hidden, half), lambda i, lane_ref: (0, lane_ref[0])),
            ],
            out_specs=pl.BlockSpec((block_rows * fold, HEAD_WIDTH), lambda i, lane_ref: (i, 0)),
            scratch_shapes=[pltpu.VMEM((block_rows * fold, HEAD_WIDTH), jnp.float32)],
        ),
        out_shape=jax.ShapeDtypeStruct((rows * fold, HEAD_WIDTH), jnp.bfloat16),
        interpret=interpret,
    )(lane, act_mine, act_other, down_mat, down_other)


def swap_pair(x):
    return lax.ppermute(x, "tensor", [(0, 1), (1, 0)])


def per_device(
    queries,
    fresh_keys,
    fresh_values,
    resident_keys,
    resident_values,
    out_weight,
    residual,
    norm_gain,
    expert_ids,
    gates,
    w_gate,
    w_up,
    w_down,
):
    tokens_here = residual.shape[0]
    lane = lax.axis_index("tensor")
    half = D // lax.axis_size("tensor")
    groups = lax.axis_size("dp")
    attended = attend_kernel(queries, fresh_keys, fresh_values, resident_keys, resident_values)

    here = lax.axis_index("dp")
    blocks = [jnp.dot(attended, out_weight, preferred_element_type=jnp.float32)]
    for shift in range(1, groups):
        onward = [(i, (i + shift) % groups) for i in range(groups)]
        backward = [(i, (i - shift) % groups) for i in range(groups)]
        arrived = lax.ppermute(attended, "dp", onward)
        product = jnp.dot(arrived, out_weight, preferred_element_type=jnp.float32)
        blocks.append(lax.ppermute(product, "dp", backward))
    stacked = jnp.stack(blocks)
    order = (jnp.arange(groups) - here) % groups
    mine = stacked[order].transpose(1, 0, 2).reshape(tokens_here, D)
    summed = mine + swap_pair(mine)
    hidden = residual.astype(jnp.float32) + summed
    mean_square = jnp.mean(hidden * hidden, axis=-1, keepdims=True)
    normed = (hidden * lax.rsqrt(mean_square + 1e-06) * norm_gain).astype(jnp.bfloat16)
    hidden_half = lax.dynamic_slice_in_dim(hidden, lane * half, half, 1)
    normed_half = lax.dynamic_slice_in_dim(normed, lane * half, half, 1)

    owners = lax.axis_size("dp") * lax.axis_size("expert")
    onehot = (expert_ids[:, :, None] == jnp.arange(owners)[None, None, :]).astype(jnp.int32)
    per_token = jnp.sum(onehot, axis=1)
    before = jnp.cumsum(per_token, axis=0) - per_token
    slot = jnp.sum(onehot * before[:, None, :], axis=-1)
    code = expert_ids * CAP + slot
    pick = (code[:, :, None] == jnp.arange(owners * CAP)[None, None, :]).astype(jnp.bfloat16)
    spread = jnp.sum(pick, axis=1)
    lanes = 128
    width = half // lanes
    outgoing = jnp.einsum(
        "tr,tjl->rjl", spread, normed_half.reshape(tokens_here, width, lanes),
        preferred_element_type=jnp.float32,
    ).astype(jnp.bfloat16)
    received = lax.all_to_all(
        outgoing.reshape(owners, CAP * width, lanes), ("dp", "expert"), split_axis=0, concat_axis=0, tiled=True
    ).reshape(owners * CAP * width, lanes)
    other = swap_pair(received)
    lane_id = lane.astype(jnp.int32).reshape(1)
    down_other = swap_pair(w_down[0])
    act = gate_up(lane_id, received, other, w_gate[0], w_up[0])
    expert_out = down(lane_id, act, swap_pair(act), w_down[0], down_other)

    returned = lax.all_to_all(
        expert_out.reshape(owners, CAP * width, lanes), ("dp", "expert"), split_axis=0, concat_axis=0, tiled=True
    ).reshape(owners * CAP, width, lanes)
    spread_gates = jnp.sum(gates[:, :, None] * pick.astype(jnp.float32), axis=1)
    first_part = spread_gates.astype(jnp.bfloat16)
    rest = spread_gates - first_part.astype(jnp.float32)
    second_part = rest.astype(jnp.bfloat16)
    third_part = (rest - second_part.astype(jnp.float32)).astype(jnp.bfloat16)
    parts = jnp.concatenate([first_part, second_part, third_part], axis=0)
    combined = jnp.einsum("sr,rjl->sjl", parts, returned, preferred_element_type=jnp.float32)
    moe = jnp.sum(combined.reshape(3, tokens_here, width, lanes), axis=0).reshape(tokens_here, half)
    return (hidden_half + moe).astype(jnp.bfloat16)


def solution(mesh):
    return jax.shard_map(
        per_device,
        mesh=mesh,
        in_specs=(
            P(("dp", "expert"), "tensor"),
            P(("dp", "expert"), "tensor"),
            P(("dp", "expert"), "tensor"),
            P(("dp", "expert"), None, "tensor"),
            P(("dp", "expert"), None, "tensor"),
            P("tensor", "dp"),
            P(("dp", "expert"), None),
            P(),
            P(("dp", "expert"), None),
            P(("dp", "expert"), None),
            P(("dp", "expert"), None, "tensor"),
            P(("dp", "expert"), None, "tensor"),
            P(("dp", "expert"), "tensor", None),
        ),
        out_specs=P(("dp", "expert"), "tensor"),
        check_vma=False,
    )
```

```python
import jax
import jax.numpy as jnp
from jax import lax
from jax.experimental import pallas as pl
from jax.experimental.pallas import tpu as pltpu
from jax.sharding import PartitionSpec as P

D = 2048
HEAD_WIDTH = 128
CAP = 6


def attend_local(queries, fresh_keys, fresh_values, resident_keys, resident_values):
    tokens_here = queries.shape[0]
    kv_here = fresh_keys.shape[1] // HEAD_WIDTH
    query_group = queries.shape[1] // HEAD_WIDTH // kv_here
    context = resident_keys.shape[1]
    query_rows = queries.reshape(tokens_here, kv_here, query_group, HEAD_WIDTH)
    joined_keys = jnp.concatenate([resident_keys[0], fresh_keys], 0).reshape(
        context + tokens_here, kv_here, HEAD_WIDTH
    )
    joined_values = jnp.concatenate([resident_values[0], fresh_values], 0).reshape(
        context + tokens_here, kv_here, HEAD_WIDTH
    )
    score = jnp.einsum(
        "tjgd,sjd->jgts", query_rows, joined_keys, preferred_element_type=jnp.float32
    ) * HEAD_WIDTH ** (-0.5)
    places = jnp.arange(context + tokens_here)
    rows = jnp.arange(tokens_here)
    allowed = (places[None, :] < context) | (places[None, :] - context <= rows[:, None])
    score = jnp.where(allowed, score, jnp.float32(-1e30))
    top_score = jnp.max(score, axis=-1, keepdims=True)
    weight = jnp.exp(score - top_score)
    probs = (weight / jnp.sum(weight, axis=-1, keepdims=True)).astype(jnp.bfloat16)
    attended = jnp.einsum(
        "jgts,sjd->tjgd", probs, joined_values, preferred_element_type=jnp.float32
    )
    return attended.reshape(tokens_here, -1).astype(jnp.bfloat16)


def attention_kernel(q_ref, kn_ref, vn_ref, kr_ref, vr_ref, o_ref):
    tokens = q_ref.shape[0]
    group = q_ref.shape[1] // HEAD_WIDTH
    k_res = kr_ref[0]
    v_res = vr_ref[0]
    k_new = kn_ref[...]
    v_new = vn_ref[...]
    q = jnp.concatenate(
        [q_ref[:, g * HEAD_WIDTH:(g + 1) * HEAD_WIDTH] for g in range(group)], axis=0
    )
    rows = lax.broadcasted_iota(jnp.int32, (group * tokens, tokens), 0) % tokens
    cols = lax.broadcasted_iota(jnp.int32, (group * tokens, tokens), 1)
    visible = cols <= rows
    scale = HEAD_WIDTH ** (-0.5)
    dims = (((1,), (1,)), ((), ()))
    s_res = lax.dot_general(q, k_res, dims, preferred_element_type=jnp.float32) * scale
    s_new = lax.dot_general(q, k_new, dims, preferred_element_type=jnp.float32) * scale
    s_new = jnp.where(visible, s_new, jnp.float32(-1e30))
    top = jnp.maximum(
        jnp.max(s_res, axis=1, keepdims=True), jnp.max(s_new, axis=1, keepdims=True)
    )
    w_res = jnp.exp(s_res - top)
    w_new = jnp.exp(s_new - top)
    total = jnp.sum(w_res, axis=1, keepdims=True) + jnp.sum(w_new, axis=1, keepdims=True)
    inverse = 1.0 / total
    p_res = (w_res * inverse).astype(jnp.bfloat16)
    p_new = (w_new * inverse).astype(jnp.bfloat16)
    out = jnp.dot(p_res, v_res, preferred_element_type=jnp.float32) + jnp.dot(
        p_new, v_new, preferred_element_type=jnp.float32
    )
    out = out.astype(o_ref.dtype)
    for g in range(group):
        o_ref[:, g * HEAD_WIDTH:(g + 1) * HEAD_WIDTH] = out[g * tokens:(g + 1) * tokens]


def attend_kernel(queries, fresh_keys, fresh_values, resident_keys, resident_values, interpret=False):
    tokens = queries.shape[0]
    kv_here = fresh_keys.shape[1] // HEAD_WIDTH
    width = queries.shape[1] // kv_here
    context = resident_keys.shape[1]
    return pl.pallas_call(
        attention_kernel,
        grid=(kv_here,),
        in_specs=[
            pl.BlockSpec((tokens, width), lambda j: (0, j)),
            pl.BlockSpec((tokens, HEAD_WIDTH), lambda j: (0, j)),
            pl.BlockSpec((tokens, HEAD_WIDTH), lambda j: (0, j)),
            pl.BlockSpec((1, context, HEAD_WIDTH), lambda j: (0, 0, j)),
            pl.BlockSpec((1, context, HEAD_WIDTH), lambda j: (0, 0, j)),
        ],
        out_specs=pl.BlockSpec((tokens, width), lambda j: (0, j)),
        out_shape=jax.ShapeDtypeStruct(queries.shape, jnp.bfloat16),
        interpret=interpret,
    )(queries, fresh_keys, fresh_values, resident_keys, resident_values)


def gate_up_kernel(lane_ref, mine_ref, other_ref, g_own, g_other, u_own, u_other, act_ref):
    fold = g_own.shape[0] // HEAD_WIDTH
    rows = act_ref.shape[0]
    x_mine = jnp.concatenate(
        [mine_ref[pl.ds(j, rows, stride=fold), :] for j in range(fold)], axis=1
    )
    x_other = jnp.concatenate(
        [other_ref[pl.ds(j, rows, stride=fold), :] for j in range(fold)], axis=1
    )
    gate = jnp.dot(x_mine, g_own[...], preferred_element_type=jnp.float32) + jnp.dot(
        x_other, g_other[...], preferred_element_type=jnp.float32
    )
    up = jnp.dot(x_mine, u_own[...], preferred_element_type=jnp.float32) + jnp.dot(
        x_other, u_other[...], preferred_element_type=jnp.float32
    )
    act_ref[...] = (gate / (1.0 + jnp.exp(-gate)) * up).astype(act_ref.dtype)


def down_kernel(lane_ref, act_mine, act_other, d_own, d_other, out_ref, fold_ref):
    fold = d_own.shape[1] // HEAD_WIDTH
    rows = act_mine.shape[0]
    out = jnp.dot(act_mine[...], d_own[...], preferred_element_type=jnp.float32) + jnp.dot(
        act_other[...], d_other[...], preferred_element_type=jnp.float32
    )
    for j in range(fold):
        fold_ref[pl.ds(j, rows, stride=fold), :] = out[:, j * HEAD_WIDTH:(j + 1) * HEAD_WIDTH]
    out_ref[...] = fold_ref[...].astype(out_ref.dtype)


def gate_up(lane, mine, other, gate_mat, up_mat, block_rows=256, interpret=False):
    folded, lanes = mine.shape
    half, hidden = gate_mat.shape[0] // 2, gate_mat.shape[1]
    fold = half // lanes
    rows = folded // fold
    act_spec = pl.BlockSpec((block_rows * fold, lanes), lambda i, lane_ref: (i, 0))
    own_rows = pl.BlockSpec((half, hidden), lambda i, lane_ref: (lane_ref[0], 0))
    other_rows = pl.BlockSpec((half, hidden), lambda i, lane_ref: (1 - lane_ref[0], 0))
    return pl.pallas_call(
        gate_up_kernel,
        grid_spec=pltpu.PrefetchScalarGridSpec(
            num_scalar_prefetch=1,
            grid=(rows // block_rows,),
            in_specs=[act_spec, act_spec, own_rows, other_rows, own_rows, other_rows],
            out_specs=pl.BlockSpec((block_rows, hidden), lambda i, lane_ref: (i, 0)),
        ),
        out_shape=jax.ShapeDtypeStruct((rows, hidden), jnp.bfloat16),
        interpret=interpret,
    )(lane, mine, other, gate_mat, gate_mat, up_mat, up_mat)


def down(lane, act_mine, act_other, down_mat, down_other, block_rows=256, interpret=False):
    rows, hidden = act_mine.shape
    half = down_other.shape[1]
    fold = half // HEAD_WIDTH
    act_spec = pl.BlockSpec((block_rows, hidden), lambda i, lane_ref: (i, 0))
    return pl.pallas_call(
        down_kernel,
        grid_spec=pltpu.PrefetchScalarGridSpec(
            num_scalar_prefetch=1,
            grid=(rows // block_rows,),
            in_specs=[
                act_spec,
                act_spec,
                pl.BlockSpec((hidden, half), lambda i, lane_ref: (0, lane_ref[0])),
                pl.BlockSpec((hidden, half), lambda i, lane_ref: (0, 0)),
            ],
            out_specs=pl.BlockSpec((block_rows * fold, HEAD_WIDTH), lambda i, lane_ref: (i, 0)),
            scratch_shapes=[pltpu.VMEM((block_rows * fold, HEAD_WIDTH), jnp.float32)],
        ),
        out_shape=jax.ShapeDtypeStruct((rows * fold, HEAD_WIDTH), jnp.bfloat16),
        interpret=interpret,
    )(lane, act_mine, act_other, down_mat, down_other)


def swap_pair(x):
    return lax.ppermute(x, "tensor", [(0, 1), (1, 0)])


def per_device(
    queries,
    fresh_keys,
    fresh_values,
    resident_keys,
    resident_values,
    out_weight,
    residual,
    norm_gain,
    expert_ids,
    gates,
    w_gate,
    w_up,
    w_down,
):
    tokens_here = residual.shape[0]
    lane = lax.axis_index("tensor")
    half = D // lax.axis_size("tensor")
    groups = lax.axis_size("dp")
    attended = attend_kernel(queries, fresh_keys, fresh_values, resident_keys, resident_values)

    here = lax.axis_index("dp")
    blocks = [jnp.dot(attended, out_weight, preferred_element_type=jnp.float32)]
    for shift in range(1, groups):
        onward = [(i, (i + shift) % groups) for i in range(groups)]
        backward = [(i, (i - shift) % groups) for i in range(groups)]
        arrived = lax.ppermute(attended, "dp", onward)
        product = jnp.dot(arrived, out_weight, preferred_element_type=jnp.float32)
        blocks.append(lax.ppermute(product, "dp", backward))
    stacked = jnp.stack(blocks)
    order = (jnp.arange(groups) - here) % groups
    mine = stacked[order].transpose(1, 0, 2).reshape(tokens_here, D)
    summed = mine + swap_pair(mine)
    hidden = residual.astype(jnp.float32) + summed
    mean_square = jnp.mean(hidden * hidden, axis=-1, keepdims=True)
    normed = (hidden * lax.rsqrt(mean_square + 1e-06) * norm_gain).astype(jnp.bfloat16)
    hidden_half = lax.dynamic_slice_in_dim(hidden, lane * half, half, 1)
    normed_half = lax.dynamic_slice_in_dim(normed, lane * half, half, 1)

    owners = lax.axis_size("dp") * lax.axis_size("expert")
    onehot = (expert_ids[:, :, None] == jnp.arange(owners)[None, None, :]).astype(jnp.int32)
    per_token = jnp.sum(onehot, axis=1)
    before = jnp.cumsum(per_token, axis=0) - per_token
    slot = jnp.sum(onehot * before[:, None, :], axis=-1)
    code = expert_ids * CAP + slot
    pick = (code[:, :, None] == jnp.arange(owners * CAP)[None, None, :]).astype(jnp.bfloat16)
    spread = jnp.sum(pick, axis=1)
    lanes = 128
    width = half // lanes
    outgoing = jnp.einsum(
        "tr,tjl->rjl", spread, normed_half.reshape(tokens_here, width, lanes),
        preferred_element_type=jnp.float32,
    ).astype(jnp.bfloat16)
    received = lax.all_to_all(
        outgoing.reshape(owners, CAP * width, lanes), ("dp", "expert"), split_axis=0, concat_axis=0, tiled=True
    ).reshape(owners * CAP * width, lanes)
    other = swap_pair(received)
    lane_id = lane.astype(jnp.int32).reshape(1)
    down_other = swap_pair(lax.dynamic_slice_in_dim(w_down[0], (1 - lane) * half, half, 1))
    act = gate_up(lane_id, received, other, w_gate[0], w_up[0])
    expert_out = down(lane_id, act, swap_pair(act), w_down[0], down_other)

    returned = lax.all_to_all(
        expert_out.reshape(owners, CAP * width, lanes), ("dp", "expert"), split_axis=0, concat_axis=0, tiled=True
    ).reshape(owners * CAP, width, lanes)
    picked = jnp.einsum("tkr,rjl->tkjl", pick, returned, preferred_element_type=jnp.float32)
    moe = jnp.sum(gates[:, :, None, None] * picked, axis=1).reshape(tokens_here, half)
    return (hidden_half + moe).astype(jnp.bfloat16)


def solution(mesh):
    return jax.shard_map(
        per_device,
        mesh=mesh,
        in_specs=(
            P(("dp", "expert"), "tensor"),
            P(("dp", "expert"), "tensor"),
            P(("dp", "expert"), "tensor"),
            P(("dp", "expert"), None, "tensor"),
            P(("dp", "expert"), None, "tensor"),
            P("tensor", "dp"),
            P(("dp", "expert"), None),
            P(),
            P(("dp", "expert"), None),
            P(("dp", "expert"), None),
            P(("dp", "expert"), None, "tensor"),
            P(("dp", "expert"), None, "tensor"),
            P(("dp", "expert"), "tensor", None),
        ),
        out_specs=P(("dp", "expert"), "tensor"),
        check_vma=False,
    )
```

```python
import jax
import jax.numpy as jnp
from jax import lax
from jax.experimental import pallas as pl
from jax.experimental.pallas import tpu as pltpu
from jax.sharding import PartitionSpec as P

D = 2048
HEAD_WIDTH = 128
CAP = 6


def attend_local(queries, fresh_keys, fresh_values, resident_keys, resident_values):
    tokens_here = queries.shape[0]
    kv_here = fresh_keys.shape[1] // HEAD_WIDTH
    query_group = queries.shape[1] // HEAD_WIDTH // kv_here
    context = resident_keys.shape[1]
    query_rows = queries.reshape(tokens_here, kv_here, query_group, HEAD_WIDTH)
    joined_keys = jnp.concatenate([resident_keys[0], fresh_keys], 0).reshape(
        context + tokens_here, kv_here, HEAD_WIDTH
    )
    joined_values = jnp.concatenate([resident_values[0], fresh_values], 0).reshape(
        context + tokens_here, kv_here, HEAD_WIDTH
    )
    score = jnp.einsum(
        "tjgd,sjd->jgts", query_rows, joined_keys, preferred_element_type=jnp.float32
    ) * HEAD_WIDTH ** (-0.5)
    places = jnp.arange(context + tokens_here)
    rows = jnp.arange(tokens_here)
    allowed = (places[None, :] < context) | (places[None, :] - context <= rows[:, None])
    score = jnp.where(allowed, score, jnp.float32(-1e30))
    top_score = jnp.max(score, axis=-1, keepdims=True)
    weight = jnp.exp(score - top_score)
    probs = (weight / jnp.sum(weight, axis=-1, keepdims=True)).astype(jnp.bfloat16)
    attended = jnp.einsum(
        "jgts,sjd->tjgd", probs, joined_values, preferred_element_type=jnp.float32
    )
    return attended.reshape(tokens_here, -1).astype(jnp.bfloat16)


def attention_kernel(q_ref, kn_ref, vn_ref, kr_ref, vr_ref, o_ref):
    tokens = q_ref.shape[0]
    group = q_ref.shape[1] // HEAD_WIDTH
    k_res = kr_ref[0]
    v_res = vr_ref[0]
    k_new = kn_ref[...]
    v_new = vn_ref[...]
    q = jnp.concatenate(
        [q_ref[:, g * HEAD_WIDTH:(g + 1) * HEAD_WIDTH] for g in range(group)], axis=0
    )
    rows = lax.broadcasted_iota(jnp.int32, (group * tokens, tokens), 0) % tokens
    cols = lax.broadcasted_iota(jnp.int32, (group * tokens, tokens), 1)
    visible = cols <= rows
    scale = HEAD_WIDTH ** (-0.5)
    dims = (((1,), (1,)), ((), ()))
    s_res = lax.dot_general(q, k_res, dims, preferred_element_type=jnp.float32) * scale
    s_new = lax.dot_general(q, k_new, dims, preferred_element_type=jnp.float32) * scale
    s_new = jnp.where(visible, s_new, jnp.float32(-1e30))
    top = jnp.maximum(
        jnp.max(s_res, axis=1, keepdims=True), jnp.max(s_new, axis=1, keepdims=True)
    )
    w_res = jnp.exp(s_res - top)
    w_new = jnp.exp(s_new - top)
    total = jnp.sum(w_res, axis=1, keepdims=True) + jnp.sum(w_new, axis=1, keepdims=True)
    inverse = 1.0 / total
    p_res = (w_res * inverse).astype(jnp.bfloat16)
    p_new = (w_new * inverse).astype(jnp.bfloat16)
    out = jnp.dot(p_res, v_res, preferred_element_type=jnp.float32) + jnp.dot(
        p_new, v_new, preferred_element_type=jnp.float32
    )
    out = out.astype(o_ref.dtype)
    for g in range(group):
        o_ref[:, g * HEAD_WIDTH:(g + 1) * HEAD_WIDTH] = out[g * tokens:(g + 1) * tokens]


def attend_kernel(queries, fresh_keys, fresh_values, resident_keys, resident_values, interpret=False):
    tokens = queries.shape[0]
    kv_here = fresh_keys.shape[1] // HEAD_WIDTH
    width = queries.shape[1] // kv_here
    context = resident_keys.shape[1]
    return pl.pallas_call(
        attention_kernel,
        grid=(kv_here,),
        in_specs=[
            pl.BlockSpec((tokens, width), lambda j: (0, j)),
            pl.BlockSpec((tokens, HEAD_WIDTH), lambda j: (0, j)),
            pl.BlockSpec((tokens, HEAD_WIDTH), lambda j: (0, j)),
            pl.BlockSpec((1, context, HEAD_WIDTH), lambda j: (0, 0, j)),
            pl.BlockSpec((1, context, HEAD_WIDTH), lambda j: (0, 0, j)),
        ],
        out_specs=pl.BlockSpec((tokens, width), lambda j: (0, j)),
        out_shape=jax.ShapeDtypeStruct(queries.shape, jnp.bfloat16),
        interpret=interpret,
    )(queries, fresh_keys, fresh_values, resident_keys, resident_values)


def gate_up_kernel(lane_ref, mine_ref, other_ref, g_own, g_other, u_own, u_other, act_ref):
    fold = g_own.shape[0] // HEAD_WIDTH
    rows = act_ref.shape[0]
    x_mine = jnp.concatenate(
        [mine_ref[pl.ds(j, rows, stride=fold), :] for j in range(fold)], axis=1
    )
    x_other = jnp.concatenate(
        [other_ref[pl.ds(j, rows, stride=fold), :] for j in range(fold)], axis=1
    )
    gate = jnp.dot(x_mine, g_own[...], preferred_element_type=jnp.float32) + jnp.dot(
        x_other, g_other[...], preferred_element_type=jnp.float32
    )
    up = jnp.dot(x_mine, u_own[...], preferred_element_type=jnp.float32) + jnp.dot(
        x_other, u_other[...], preferred_element_type=jnp.float32
    )
    act_ref[...] = (gate / (1.0 + jnp.exp(-gate)) * up).astype(act_ref.dtype)


def down_kernel(lane_ref, act_mine, act_other, d_own, d_other, out_ref, fold_ref):
    fold = d_own.shape[1] // HEAD_WIDTH
    rows = act_mine.shape[0]
    out = jnp.dot(act_mine[...], d_own[...], preferred_element_type=jnp.float32) + jnp.dot(
        act_other[...], d_other[...], preferred_element_type=jnp.float32
    )
    for j in range(fold):
        fold_ref[pl.ds(j, rows, stride=fold), :] = out[:, j * HEAD_WIDTH:(j + 1) * HEAD_WIDTH]
    out_ref[...] = fold_ref[...].astype(out_ref.dtype)


def gate_up(lane, mine, other, gate_mat, up_mat, block_rows=256, interpret=False):
    folded, lanes = mine.shape
    half, hidden = gate_mat.shape[0] // 2, gate_mat.shape[1]
    fold = half // lanes
    rows = folded // fold
    act_spec = pl.BlockSpec((block_rows * fold, lanes), lambda i, lane_ref: (i, 0))
    own_rows = pl.BlockSpec((half, hidden), lambda i, lane_ref: (lane_ref[0], 0))
    other_rows = pl.BlockSpec((half, hidden), lambda i, lane_ref: (1 - lane_ref[0], 0))
    return pl.pallas_call(
        gate_up_kernel,
        grid_spec=pltpu.PrefetchScalarGridSpec(
            num_scalar_prefetch=1,
            grid=(rows // block_rows,),
            in_specs=[act_spec, act_spec, own_rows, other_rows, own_rows, other_rows],
            out_specs=pl.BlockSpec((block_rows, hidden), lambda i, lane_ref: (i, 0)),
        ),
        out_shape=jax.ShapeDtypeStruct((rows, hidden), jnp.bfloat16),
        interpret=interpret,
    )(lane, mine, other, gate_mat, gate_mat, up_mat, up_mat)


def down(lane, act_mine, act_other, down_mat, down_other, block_rows=256, interpret=False):
    rows, hidden = act_mine.shape
    half = down_other.shape[1]
    fold = half // HEAD_WIDTH
    act_spec = pl.BlockSpec((block_rows, hidden), lambda i, lane_ref: (i, 0))
    return pl.pallas_call(
        down_kernel,
        grid_spec=pltpu.PrefetchScalarGridSpec(
            num_scalar_prefetch=1,
            grid=(rows // block_rows,),
            in_specs=[
                act_spec,
                act_spec,
                pl.BlockSpec((hidden, half), lambda i, lane_ref: (0, lane_ref[0])),
                pl.BlockSpec((hidden, half), lambda i, lane_ref: (0, 0)),
            ],
            out_specs=pl.BlockSpec((block_rows * fold, HEAD_WIDTH), lambda i, lane_ref: (i, 0)),
            scratch_shapes=[pltpu.VMEM((block_rows * fold, HEAD_WIDTH), jnp.float32)],
        ),
        out_shape=jax.ShapeDtypeStruct((rows * fold, HEAD_WIDTH), jnp.bfloat16),
        interpret=interpret,
    )(lane, act_mine, act_other, down_mat, down_other)


def combine_kernel(code_ref, gates_ref, ret_ref, hid_ref, out_ref):
    fold = hid_ref.shape[1] // HEAD_WIDTH
    rows = ret_ref.shape[0] // fold
    tokens, top = code_ref.shape
    places = lax.broadcasted_iota(jnp.int32, (tokens, rows), 1)
    code = code_ref[...]
    gates = gates_ref[...]
    spread = jnp.zeros((tokens, rows), jnp.float32)
    for k in range(top):
        spread = spread + jnp.where(places == code[:, k:k + 1], gates[:, k:k + 1], jnp.float32(0.0))
    first = spread.astype(jnp.bfloat16)
    rest = spread - first.astype(jnp.float32)
    second = rest.astype(jnp.bfloat16)
    third = (rest - second.astype(jnp.float32)).astype(jnp.bfloat16)
    returned = jnp.concatenate(
        [ret_ref[pl.ds(j, rows, stride=fold), :] for j in range(fold)], axis=1
    )
    moe = jnp.dot(first, returned, preferred_element_type=jnp.float32)
    moe = moe + jnp.dot(second, returned, preferred_element_type=jnp.float32)
    moe = moe + jnp.dot(third, returned, preferred_element_type=jnp.float32)
    out_ref[...] = (hid_ref[...] + moe).astype(out_ref.dtype)


def combine(code, gates, returned, hidden_half, interpret=False):
    return pl.pallas_call(
        combine_kernel,
        out_shape=jax.ShapeDtypeStruct(hidden_half.shape, jnp.bfloat16),
        interpret=interpret,
    )(code, gates, returned, hidden_half)


def swap_pair(x):
    return lax.ppermute(x, "tensor", [(0, 1), (1, 0)])


def per_device(
    queries,
    fresh_keys,
    fresh_values,
    resident_keys,
    resident_values,
    out_weight,
    residual,
    norm_gain,
    expert_ids,
    gates,
    w_gate,
    w_up,
    w_down,
):
    tokens_here = residual.shape[0]
    lane = lax.axis_index("tensor")
    half = D // lax.axis_size("tensor")
    groups = lax.axis_size("dp")
    attended = attend_kernel(queries, fresh_keys, fresh_values, resident_keys, resident_values)

    here = lax.axis_index("dp")
    blocks = [jnp.dot(attended, out_weight, preferred_element_type=jnp.float32)]
    for shift in range(1, groups):
        onward = [(i, (i + shift) % groups) for i in range(groups)]
        backward = [(i, (i - shift) % groups) for i in range(groups)]
        arrived = lax.ppermute(attended, "dp", onward)
        product = jnp.dot(arrived, out_weight, preferred_element_type=jnp.float32)
        blocks.append(lax.ppermute(product, "dp", backward))
    stacked = jnp.stack(blocks)
    order = (jnp.arange(groups) - here) % groups
    mine = stacked[order].transpose(1, 0, 2).reshape(tokens_here, D)
    summed = mine + swap_pair(mine)
    hidden = residual.astype(jnp.float32) + summed
    mean_square = jnp.mean(hidden * hidden, axis=-1, keepdims=True)
    normed = (hidden * lax.rsqrt(mean_square + 1e-06) * norm_gain).astype(jnp.bfloat16)
    hidden_half = lax.dynamic_slice_in_dim(hidden, lane * half, half, 1)
    normed_half = lax.dynamic_slice_in_dim(normed, lane * half, half, 1)

    owners = lax.axis_size("dp") * lax.axis_size("expert")
    onehot = (expert_ids[:, :, None] == jnp.arange(owners)[None, None, :]).astype(jnp.int32)
    per_token = jnp.sum(onehot, axis=1)
    before = jnp.cumsum(per_token, axis=0) - per_token
    slot = jnp.sum(onehot * before[:, None, :], axis=-1)
    code = expert_ids * CAP + slot
    pick = (code[:, :, None] == jnp.arange(owners * CAP)[None, None, :]).astype(jnp.bfloat16)
    spread = jnp.sum(pick, axis=1)
    lanes = 128
    width = half // lanes
    outgoing = jnp.einsum(
        "tr,tjl->rjl", spread, normed_half.reshape(tokens_here, width, lanes),
        preferred_element_type=jnp.float32,
    ).astype(jnp.bfloat16)
    received = lax.all_to_all(
        outgoing.reshape(owners, CAP * width, lanes), ("dp", "expert"), split_axis=0, concat_axis=0, tiled=True
    ).reshape(owners * CAP * width, lanes)
    other = swap_pair(received)
    lane_id = lane.astype(jnp.int32).reshape(1)
    down_other = swap_pair(lax.dynamic_slice_in_dim(w_down[0], (1 - lane) * half, half, 1))
    act = gate_up(lane_id, received, other, w_gate[0], w_up[0])
    expert_out = down(lane_id, act, swap_pair(act), w_down[0], down_other)

    returned = lax.all_to_all(
        expert_out.reshape(owners, CAP * width, lanes), ("dp", "expert"), split_axis=0, concat_axis=0, tiled=True
    ).reshape(owners * CAP * width, lanes)
    return combine(code, gates, returned, hidden_half)


def solution(mesh):
    return jax.shard_map(
        per_device,
        mesh=mesh,
        in_specs=(
            P(("dp", "expert"), "tensor"),
            P(("dp", "expert"), "tensor"),
            P(("dp", "expert"), "tensor"),
            P(("dp", "expert"), None, "tensor"),
            P(("dp", "expert"), None, "tensor"),
            P("tensor", "dp"),
            P(("dp", "expert"), None),
            P(),
            P(("dp", "expert"), None),
            P(("dp", "expert"), None),
            P(("dp", "expert"), None, "tensor"),
            P(("dp", "expert"), None, "tensor"),
            P(("dp", "expert"), "tensor", None),
        ),
        out_specs=P(("dp", "expert"), "tensor"),
        check_vma=False,
    )
```

```python
import jax
import jax.numpy as jnp
from jax import lax
from jax.experimental import pallas as pl
from jax.experimental.pallas import tpu as pltpu
from jax.sharding import PartitionSpec as P

D = 2048
HEAD_WIDTH = 128
CAP = 6


def attend_local(queries, fresh_keys, fresh_values, resident_keys, resident_values):
    tokens_here = queries.shape[0]
    kv_here = fresh_keys.shape[1] // HEAD_WIDTH
    query_group = queries.shape[1] // HEAD_WIDTH // kv_here
    context = resident_keys.shape[1]
    query_rows = queries.reshape(tokens_here, kv_here, query_group, HEAD_WIDTH)
    joined_keys = jnp.concatenate([resident_keys[0], fresh_keys], 0).reshape(
        context + tokens_here, kv_here, HEAD_WIDTH
    )
    joined_values = jnp.concatenate([resident_values[0], fresh_values], 0).reshape(
        context + tokens_here, kv_here, HEAD_WIDTH
    )
    score = jnp.einsum(
        "tjgd,sjd->jgts", query_rows, joined_keys, preferred_element_type=jnp.float32
    ) * HEAD_WIDTH ** (-0.5)
    places = jnp.arange(context + tokens_here)
    rows = jnp.arange(tokens_here)
    allowed = (places[None, :] < context) | (places[None, :] - context <= rows[:, None])
    score = jnp.where(allowed, score, jnp.float32(-1e30))
    top_score = jnp.max(score, axis=-1, keepdims=True)
    weight = jnp.exp(score - top_score)
    probs = (weight / jnp.sum(weight, axis=-1, keepdims=True)).astype(jnp.bfloat16)
    attended = jnp.einsum(
        "jgts,sjd->tjgd", probs, joined_values, preferred_element_type=jnp.float32
    )
    return attended.reshape(tokens_here, -1).astype(jnp.bfloat16)


def attention_kernel(q_ref, kn_ref, vn_ref, kr_ref, vr_ref, o_ref):
    tokens = q_ref.shape[0]
    group = q_ref.shape[1] // HEAD_WIDTH
    k_res = kr_ref[0]
    v_res = vr_ref[0]
    k_new = kn_ref[...]
    v_new = vn_ref[...]
    q = jnp.concatenate(
        [q_ref[:, g * HEAD_WIDTH:(g + 1) * HEAD_WIDTH] for g in range(group)], axis=0
    )
    rows = lax.broadcasted_iota(jnp.int32, (group * tokens, tokens), 0) % tokens
    cols = lax.broadcasted_iota(jnp.int32, (group * tokens, tokens), 1)
    visible = cols <= rows
    scale = HEAD_WIDTH ** (-0.5)
    dims = (((1,), (1,)), ((), ()))
    s_res = lax.dot_general(q, k_res, dims, preferred_element_type=jnp.float32) * scale
    s_new = lax.dot_general(q, k_new, dims, preferred_element_type=jnp.float32) * scale
    s_new = jnp.where(visible, s_new, jnp.float32(-1e30))
    top = jnp.maximum(
        jnp.max(s_res, axis=1, keepdims=True), jnp.max(s_new, axis=1, keepdims=True)
    )
    w_res = jnp.exp(s_res - top)
    w_new = jnp.exp(s_new - top)
    total = jnp.sum(w_res, axis=1, keepdims=True) + jnp.sum(w_new, axis=1, keepdims=True)
    inverse = 1.0 / total
    p_res = (w_res * inverse).astype(jnp.bfloat16)
    p_new = (w_new * inverse).astype(jnp.bfloat16)
    out = jnp.dot(p_res, v_res, preferred_element_type=jnp.float32) + jnp.dot(
        p_new, v_new, preferred_element_type=jnp.float32
    )
    out = out.astype(o_ref.dtype)
    for g in range(group):
        o_ref[:, g * HEAD_WIDTH:(g + 1) * HEAD_WIDTH] = out[g * tokens:(g + 1) * tokens]


def attend_kernel(queries, fresh_keys, fresh_values, resident_keys, resident_values, interpret=False):
    tokens = queries.shape[0]
    kv_here = fresh_keys.shape[1] // HEAD_WIDTH
    width = queries.shape[1] // kv_here
    context = resident_keys.shape[1]
    return pl.pallas_call(
        attention_kernel,
        grid=(kv_here,),
        in_specs=[
            pl.BlockSpec((tokens, width), lambda j: (0, j)),
            pl.BlockSpec((tokens, HEAD_WIDTH), lambda j: (0, j)),
            pl.BlockSpec((tokens, HEAD_WIDTH), lambda j: (0, j)),
            pl.BlockSpec((1, context, HEAD_WIDTH), lambda j: (0, 0, j)),
            pl.BlockSpec((1, context, HEAD_WIDTH), lambda j: (0, 0, j)),
        ],
        out_specs=pl.BlockSpec((tokens, width), lambda j: (0, j)),
        out_shape=jax.ShapeDtypeStruct(queries.shape, jnp.bfloat16),
        interpret=interpret,
    )(queries, fresh_keys, fresh_values, resident_keys, resident_values)


def gate_up_kernel(lane_ref, mine_ref, other_ref, g_own, g_other, u_own, u_other, act_ref):
    fold = g_own.shape[0] // HEAD_WIDTH
    rows = act_ref.shape[0]
    x_mine = jnp.concatenate(
        [mine_ref[pl.ds(j, rows, stride=fold), :] for j in range(fold)], axis=1
    )
    x_other = jnp.concatenate(
        [other_ref[pl.ds(j, rows, stride=fold), :] for j in range(fold)], axis=1
    )
    gate = jnp.dot(x_mine, g_own[...], preferred_element_type=jnp.float32) + jnp.dot(
        x_other, g_other[...], preferred_element_type=jnp.float32
    )
    up = jnp.dot(x_mine, u_own[...], preferred_element_type=jnp.float32) + jnp.dot(
        x_other, u_other[...], preferred_element_type=jnp.float32
    )
    act_ref[...] = (gate / (1.0 + jnp.exp(-gate)) * up).astype(act_ref.dtype)


def down_kernel(lane_ref, act_mine, act_other, d_own, d_other, out_ref, fold_ref):
    fold = d_own.shape[1] // HEAD_WIDTH
    rows = act_mine.shape[0]
    out = jnp.dot(act_mine[...], d_own[...], preferred_element_type=jnp.float32) + jnp.dot(
        act_other[...], d_other[...], preferred_element_type=jnp.float32
    )
    for j in range(fold):
        fold_ref[pl.ds(j, rows, stride=fold), :] = out[:, j * HEAD_WIDTH:(j + 1) * HEAD_WIDTH]
    out_ref[...] = fold_ref[...].astype(out_ref.dtype)


def gate_up(lane, mine, other, gate_mat, up_mat, block_rows=256, interpret=False):
    folded, lanes = mine.shape
    half, hidden = gate_mat.shape[0] // 2, gate_mat.shape[1]
    fold = half // lanes
    rows = folded // fold
    act_spec = pl.BlockSpec((block_rows * fold, lanes), lambda i, lane_ref: (i, 0))
    own_rows = pl.BlockSpec((half, hidden), lambda i, lane_ref: (lane_ref[0], 0))
    other_rows = pl.BlockSpec((half, hidden), lambda i, lane_ref: (1 - lane_ref[0], 0))
    return pl.pallas_call(
        gate_up_kernel,
        grid_spec=pltpu.PrefetchScalarGridSpec(
            num_scalar_prefetch=1,
            grid=(rows // block_rows,),
            in_specs=[act_spec, act_spec, own_rows, other_rows, own_rows, other_rows],
            out_specs=pl.BlockSpec((block_rows, hidden), lambda i, lane_ref: (i, 0)),
        ),
        out_shape=jax.ShapeDtypeStruct((rows, hidden), jnp.bfloat16),
        interpret=interpret,
    )(lane, mine, other, gate_mat, gate_mat, up_mat, up_mat)


def down(lane, act_mine, act_other, down_mat, down_other, block_rows=256, interpret=False):
    rows, hidden = act_mine.shape
    half = down_other.shape[1]
    fold = half // HEAD_WIDTH
    act_spec = pl.BlockSpec((block_rows, hidden), lambda i, lane_ref: (i, 0))
    return pl.pallas_call(
        down_kernel,
        grid_spec=pltpu.PrefetchScalarGridSpec(
            num_scalar_prefetch=1,
            grid=(rows // block_rows,),
            in_specs=[
                act_spec,
                act_spec,
                pl.BlockSpec((hidden, half), lambda i, lane_ref: (0, lane_ref[0])),
                pl.BlockSpec((hidden, half), lambda i, lane_ref: (0, 0)),
            ],
            out_specs=pl.BlockSpec((block_rows * fold, HEAD_WIDTH), lambda i, lane_ref: (i, 0)),
            scratch_shapes=[pltpu.VMEM((block_rows * fold, HEAD_WIDTH), jnp.float32)],
        ),
        out_shape=jax.ShapeDtypeStruct((rows * fold, HEAD_WIDTH), jnp.bfloat16),
        interpret=interpret,
    )(lane, act_mine, act_other, down_mat, down_other)


def combine_kernel(code_ref, gates_ref, ret_ref, hid_ref, out_ref):
    fold = hid_ref.shape[1] // HEAD_WIDTH
    rows = ret_ref.shape[0] // fold
    tokens, top = code_ref.shape
    places = lax.broadcasted_iota(jnp.int32, (tokens, rows), 1)
    code = code_ref[...]
    gates = gates_ref[...]
    spread = jnp.zeros((tokens, rows), jnp.float32)
    for k in range(top):
        spread = spread + jnp.where(places == code[:, k:k + 1], gates[:, k:k + 1], jnp.float32(0.0))
    first = spread.astype(jnp.bfloat16)
    rest = spread - first.astype(jnp.float32)
    second = rest.astype(jnp.bfloat16)
    third = (rest - second.astype(jnp.float32)).astype(jnp.bfloat16)
    returned = jnp.concatenate(
        [ret_ref[pl.ds(j, rows, stride=fold), :] for j in range(fold)], axis=1
    )
    parts = jnp.concatenate([first, second, third], axis=0)
    summed = jnp.dot(parts, returned, preferred_element_type=jnp.float32)
    moe = summed[:tokens] + summed[tokens:2 * tokens] + summed[2 * tokens:]
    out_ref[...] = (hid_ref[...] + moe).astype(out_ref.dtype)


def combine(code, gates, returned, hidden_half, interpret=False):
    return pl.pallas_call(
        combine_kernel,
        out_shape=jax.ShapeDtypeStruct(hidden_half.shape, jnp.bfloat16),
        interpret=interpret,
    )(code, gates, returned, hidden_half)


def swap_pair(x):
    return lax.ppermute(x, "tensor", [(0, 1), (1, 0)])


def per_device(
    queries,
    fresh_keys,
    fresh_values,
    resident_keys,
    resident_values,
    out_weight,
    residual,
    norm_gain,
    expert_ids,
    gates,
    w_gate,
    w_up,
    w_down,
):
    tokens_here = residual.shape[0]
    lane = lax.axis_index("tensor")
    half = D // lax.axis_size("tensor")
    groups = lax.axis_size("dp")
    attended = attend_kernel(queries, fresh_keys, fresh_values, resident_keys, resident_values)

    here = lax.axis_index("dp")
    blocks = [jnp.dot(attended, out_weight, preferred_element_type=jnp.float32)]
    for shift in range(1, groups):
        onward = [(i, (i + shift) % groups) for i in range(groups)]
        backward = [(i, (i - shift) % groups) for i in range(groups)]
        arrived = lax.ppermute(attended, "dp", onward)
        product = jnp.dot(arrived, out_weight, preferred_element_type=jnp.float32)
        blocks.append(lax.ppermute(product, "dp", backward))
    stacked = jnp.stack(blocks)
    order = (jnp.arange(groups) - here) % groups
    mine = stacked[order].transpose(1, 0, 2).reshape(tokens_here, D)
    summed = mine + swap_pair(mine)
    hidden = residual.astype(jnp.float32) + summed
    mean_square = jnp.mean(hidden * hidden, axis=-1, keepdims=True)
    normed = (hidden * lax.rsqrt(mean_square + 1e-06) * norm_gain).astype(jnp.bfloat16)
    hidden_half = lax.dynamic_slice_in_dim(hidden, lane * half, half, 1)
    normed_half = lax.dynamic_slice_in_dim(normed, lane * half, half, 1)

    owners = lax.axis_size("dp") * lax.axis_size("expert")
    onehot = (expert_ids[:, :, None] == jnp.arange(owners)[None, None, :]).astype(jnp.int32)
    per_token = jnp.sum(onehot, axis=1)
    before = jnp.cumsum(per_token, axis=0) - per_token
    slot = jnp.sum(onehot * before[:, None, :], axis=-1)
    code = expert_ids * CAP + slot
    pick = (code[:, :, None] == jnp.arange(owners * CAP)[None, None, :]).astype(jnp.bfloat16)
    spread = jnp.sum(pick, axis=1)
    lanes = 128
    width = half // lanes
    outgoing = jnp.einsum(
        "tr,tjl->rjl", spread, normed_half.reshape(tokens_here, width, lanes),
        preferred_element_type=jnp.float32,
    ).astype(jnp.bfloat16)
    received = lax.all_to_all(
        outgoing.reshape(owners, CAP * width, lanes), ("dp", "expert"), split_axis=0, concat_axis=0, tiled=True
    ).reshape(owners * CAP * width, lanes)
    other = swap_pair(received)
    lane_id = lane.astype(jnp.int32).reshape(1)
    down_other = swap_pair(lax.dynamic_slice_in_dim(w_down[0], (1 - lane) * half, half, 1))
    act = gate_up(lane_id, received, other, w_gate[0], w_up[0])
    expert_out = down(lane_id, act, swap_pair(act), w_down[0], down_other)

    returned = lax.all_to_all(
        expert_out.reshape(owners, CAP * width, lanes), ("dp", "expert"), split_axis=0, concat_axis=0, tiled=True
    ).reshape(owners * CAP * width, lanes)
    return combine(code, gates, returned, hidden_half)


def solution(mesh):
    return jax.shard_map(
        per_device,
        mesh=mesh,
        in_specs=(
            P(("dp", "expert"), "tensor"),
            P(("dp", "expert"), "tensor"),
            P(("dp", "expert"), "tensor"),
            P(("dp", "expert"), None, "tensor"),
            P(("dp", "expert"), None, "tensor"),
            P("tensor", "dp"),
            P(("dp", "expert"), None),
            P(),
            P(("dp", "expert"), None),
            P(("dp", "expert"), None),
            P(("dp", "expert"), None, "tensor"),
            P(("dp", "expert"), None, "tensor"),
            P(("dp", "expert"), "tensor", None),
        ),
        out_specs=P(("dp", "expert"), "tensor"),
        check_vma=False,
    )
```

```python
import jax
import jax.numpy as jnp
from jax import lax
from jax.experimental import pallas as pl
from jax.experimental.pallas import tpu as pltpu
from jax.sharding import PartitionSpec as P

D = 2048
HEAD_WIDTH = 128
CAP = 6


def attend_local(queries, fresh_keys, fresh_values, resident_keys, resident_values):
    tokens_here = queries.shape[0]
    kv_here = fresh_keys.shape[1] // HEAD_WIDTH
    query_group = queries.shape[1] // HEAD_WIDTH // kv_here
    context = resident_keys.shape[1]
    query_rows = queries.reshape(tokens_here, kv_here, query_group, HEAD_WIDTH)
    joined_keys = jnp.concatenate([resident_keys[0], fresh_keys], 0).reshape(
        context + tokens_here, kv_here, HEAD_WIDTH
    )
    joined_values = jnp.concatenate([resident_values[0], fresh_values], 0).reshape(
        context + tokens_here, kv_here, HEAD_WIDTH
    )
    score = jnp.einsum(
        "tjgd,sjd->jgts", query_rows, joined_keys, preferred_element_type=jnp.float32
    ) * HEAD_WIDTH ** (-0.5)
    places = jnp.arange(context + tokens_here)
    rows = jnp.arange(tokens_here)
    allowed = (places[None, :] < context) | (places[None, :] - context <= rows[:, None])
    score = jnp.where(allowed, score, jnp.float32(-1e30))
    top_score = jnp.max(score, axis=-1, keepdims=True)
    weight = jnp.exp(score - top_score)
    probs = (weight / jnp.sum(weight, axis=-1, keepdims=True)).astype(jnp.bfloat16)
    attended = jnp.einsum(
        "jgts,sjd->tjgd", probs, joined_values, preferred_element_type=jnp.float32
    )
    return attended.reshape(tokens_here, -1).astype(jnp.bfloat16)


def attention_kernel(q_ref, kn_ref, vn_ref, kr_ref, vr_ref, o_ref):
    tokens = q_ref.shape[0]
    group = q_ref.shape[1] // HEAD_WIDTH
    k_res = kr_ref[0]
    v_res = vr_ref[0]
    k_new = kn_ref[...]
    v_new = vn_ref[...]
    q = jnp.concatenate(
        [q_ref[:, g * HEAD_WIDTH:(g + 1) * HEAD_WIDTH] for g in range(group)], axis=0
    )
    rows = lax.broadcasted_iota(jnp.int32, (group * tokens, tokens), 0) % tokens
    cols = lax.broadcasted_iota(jnp.int32, (group * tokens, tokens), 1)
    visible = cols <= rows
    scale = HEAD_WIDTH ** (-0.5)
    dims = (((1,), (1,)), ((), ()))
    s_res = lax.dot_general(q, k_res, dims, preferred_element_type=jnp.float32) * scale
    s_new = lax.dot_general(q, k_new, dims, preferred_element_type=jnp.float32) * scale
    s_new = jnp.where(visible, s_new, jnp.float32(-1e30))
    top = jnp.maximum(
        jnp.max(s_res, axis=1, keepdims=True), jnp.max(s_new, axis=1, keepdims=True)
    )
    w_res = jnp.exp(s_res - top)
    w_new = jnp.exp(s_new - top)
    total = jnp.sum(w_res, axis=1, keepdims=True) + jnp.sum(w_new, axis=1, keepdims=True)
    p_res = (w_res / total).astype(jnp.bfloat16)
    p_new = (w_new / total).astype(jnp.bfloat16)
    out = jnp.dot(p_res, v_res, preferred_element_type=jnp.float32) + jnp.dot(
        p_new, v_new, preferred_element_type=jnp.float32
    )
    out = out.astype(o_ref.dtype)
    for g in range(group):
        o_ref[:, g * HEAD_WIDTH:(g + 1) * HEAD_WIDTH] = out[g * tokens:(g + 1) * tokens]


def attend_kernel(queries, fresh_keys, fresh_values, resident_keys, resident_values, interpret=False):
    tokens = queries.shape[0]
    kv_here = fresh_keys.shape[1] // HEAD_WIDTH
    width = queries.shape[1] // kv_here
    context = resident_keys.shape[1]
    return pl.pallas_call(
        attention_kernel,
        grid=(kv_here,),
        in_specs=[
            pl.BlockSpec((tokens, width), lambda j: (0, j)),
            pl.BlockSpec((tokens, HEAD_WIDTH), lambda j: (0, j)),
            pl.BlockSpec((tokens, HEAD_WIDTH), lambda j: (0, j)),
            pl.BlockSpec((1, context, HEAD_WIDTH), lambda j: (0, 0, j)),
            pl.BlockSpec((1, context, HEAD_WIDTH), lambda j: (0, 0, j)),
        ],
        out_specs=pl.BlockSpec((tokens, width), lambda j: (0, j)),
        out_shape=jax.ShapeDtypeStruct(queries.shape, jnp.bfloat16),
        interpret=interpret,
    )(queries, fresh_keys, fresh_values, resident_keys, resident_values)


def gate_up_kernel(lane_ref, mine_ref, other_ref, g_own, g_other, u_own, u_other, act_ref):
    fold = g_own.shape[0] // HEAD_WIDTH
    rows = act_ref.shape[0]
    x_mine = jnp.concatenate(
        [mine_ref[pl.ds(j, rows, stride=fold), :] for j in range(fold)], axis=1
    )
    x_other = jnp.concatenate(
        [other_ref[pl.ds(j, rows, stride=fold), :] for j in range(fold)], axis=1
    )
    gate = jnp.dot(x_mine, g_own[...], preferred_element_type=jnp.float32) + jnp.dot(
        x_other, g_other[...], preferred_element_type=jnp.float32
    )
    up = jnp.dot(x_mine, u_own[...], preferred_element_type=jnp.float32) + jnp.dot(
        x_other, u_other[...], preferred_element_type=jnp.float32
    )
    act_ref[...] = (gate / (1.0 + jnp.exp(-gate)) * up).astype(act_ref.dtype)


def down_kernel(lane_ref, act_mine, act_other, d_own, d_other, out_ref, fold_ref):
    fold = d_own.shape[1] // HEAD_WIDTH
    rows = act_mine.shape[0]
    out = jnp.dot(act_mine[...], d_own[...], preferred_element_type=jnp.float32) + jnp.dot(
        act_other[...], d_other[...], preferred_element_type=jnp.float32
    )
    for j in range(fold):
        fold_ref[pl.ds(j, rows, stride=fold), :] = out[:, j * HEAD_WIDTH:(j + 1) * HEAD_WIDTH]
    out_ref[...] = fold_ref[...].astype(out_ref.dtype)


def gate_up(lane, mine, other, gate_mat, up_mat, block_rows=256, interpret=False):
    folded, lanes = mine.shape
    half, hidden = gate_mat.shape[0] // 2, gate_mat.shape[1]
    fold = half // lanes
    rows = folded // fold
    act_spec = pl.BlockSpec((block_rows * fold, lanes), lambda i, lane_ref: (i, 0))
    own_rows = pl.BlockSpec((half, hidden), lambda i, lane_ref: (lane_ref[0], 0))
    other_rows = pl.BlockSpec((half, hidden), lambda i, lane_ref: (1 - lane_ref[0], 0))
    return pl.pallas_call(
        gate_up_kernel,
        grid_spec=pltpu.PrefetchScalarGridSpec(
            num_scalar_prefetch=1,
            grid=(rows // block_rows,),
            in_specs=[act_spec, act_spec, own_rows, other_rows, own_rows, other_rows],
            out_specs=pl.BlockSpec((block_rows, hidden), lambda i, lane_ref: (i, 0)),
        ),
        out_shape=jax.ShapeDtypeStruct((rows, hidden), jnp.bfloat16),
        interpret=interpret,
    )(lane, mine, other, gate_mat, gate_mat, up_mat, up_mat)


def down(lane, act_mine, act_other, down_mat, down_other, block_rows=256, interpret=False):
    rows, hidden = act_mine.shape
    half = down_other.shape[1]
    fold = half // HEAD_WIDTH
    act_spec = pl.BlockSpec((block_rows, hidden), lambda i, lane_ref: (i, 0))
    return pl.pallas_call(
        down_kernel,
        grid_spec=pltpu.PrefetchScalarGridSpec(
            num_scalar_prefetch=1,
            grid=(rows // block_rows,),
            in_specs=[
                act_spec,
                act_spec,
                pl.BlockSpec((hidden, half), lambda i, lane_ref: (0, lane_ref[0])),
                pl.BlockSpec((hidden, half), lambda i, lane_ref: (0, 0)),
            ],
            out_specs=pl.BlockSpec((block_rows * fold, HEAD_WIDTH), lambda i, lane_ref: (i, 0)),
            scratch_shapes=[pltpu.VMEM((block_rows * fold, HEAD_WIDTH), jnp.float32)],
        ),
        out_shape=jax.ShapeDtypeStruct((rows * fold, HEAD_WIDTH), jnp.bfloat16),
        interpret=interpret,
    )(lane, act_mine, act_other, down_mat, down_other)


def norm_dispatch_kernel(lane_ref, mine_ref, other_ref, res_ref, gain_ref, code_ref, hid_ref, out_ref, fold_ref):
    half = hid_ref.shape[1]
    fold = half // HEAD_WIDTH
    rows = fold_ref.shape[0] // fold
    top, tokens = code_ref.shape
    hidden = res_ref[...].astype(jnp.float32) + (mine_ref[...] + other_ref[...])
    mean_square = jnp.mean(hidden * hidden, axis=-1, keepdims=True)
    normed = (hidden * lax.rsqrt(mean_square + 1e-06) * gain_ref[...]).astype(jnp.bfloat16)
    first = lane_ref[0] == 0
    hid_ref[...] = jnp.where(first, hidden[:, :half], hidden[:, half:])
    normed_half = jnp.where(first, normed[:, :half], normed[:, half:])
    places = lax.broadcasted_iota(jnp.int32, (rows, tokens), 0)
    code = code_ref[...]
    spread = jnp.zeros((rows, tokens), jnp.float32)
    for k in range(top):
        spread = spread + jnp.where(places == code[k:k + 1, :], jnp.float32(1.0), jnp.float32(0.0))
    out = jnp.dot(spread.astype(jnp.bfloat16), normed_half, preferred_element_type=jnp.float32)
    for j in range(fold):
        fold_ref[pl.ds(j, rows, stride=fold), :] = out[:, j * HEAD_WIDTH:(j + 1) * HEAD_WIDTH]
    out_ref[...] = fold_ref[...].astype(out_ref.dtype)


def norm_dispatch(lane, mine, other, residual, gain, code_t, rows, interpret=False):
    tokens, width = mine.shape
    half = width // 2
    fold = half // HEAD_WIDTH
    return pl.pallas_call(
        norm_dispatch_kernel,
        grid_spec=pltpu.PrefetchScalarGridSpec(
            num_scalar_prefetch=1,
            grid=(1,),
            in_specs=[
                pl.BlockSpec((tokens, width), lambda i, lane_ref: (0, 0)),
                pl.BlockSpec((tokens, width), lambda i, lane_ref: (0, 0)),
                pl.BlockSpec((tokens, width), lambda i, lane_ref: (0, 0)),
                pl.BlockSpec((1, width), lambda i, lane_ref: (0, 0)),
                pl.BlockSpec(code_t.shape, lambda i, lane_ref: (0, 0)),
            ],
            out_specs=[
                pl.BlockSpec((tokens, half), lambda i, lane_ref: (0, 0)),
                pl.BlockSpec((rows * fold, HEAD_WIDTH), lambda i, lane_ref: (0, 0)),
            ],
            scratch_shapes=[pltpu.VMEM((rows * fold, HEAD_WIDTH), jnp.float32)],
        ),
        out_shape=[
            jax.ShapeDtypeStruct((tokens, half), jnp.float32),
            jax.ShapeDtypeStruct((rows * fold, HEAD_WIDTH), jnp.bfloat16),
        ],
        interpret=interpret,
    )(lane, mine, other, residual, gain, code_t)


def swap_pair(x):
    return lax.ppermute(x, "tensor", [(0, 1), (1, 0)])


def per_device(
    queries,
    fresh_keys,
    fresh_values,
    resident_keys,
    resident_values,
    out_weight,
    residual,
    norm_gain,
    expert_ids,
    gates,
    w_gate,
    w_up,
    w_down,
):
    tokens_here = residual.shape[0]
    lane = lax.axis_index("tensor")
    half = D // lax.axis_size("tensor")
    groups = lax.axis_size("dp")
    attended = attend_kernel(queries, fresh_keys, fresh_values, resident_keys, resident_values)

    here = lax.axis_index("dp")
    blocks = [jnp.dot(attended, out_weight, preferred_element_type=jnp.float32)]
    for shift in range(1, groups):
        onward = [(i, (i + shift) % groups) for i in range(groups)]
        backward = [(i, (i - shift) % groups) for i in range(groups)]
        arrived = lax.ppermute(attended, "dp", onward)
        product = jnp.dot(arrived, out_weight, preferred_element_type=jnp.float32)
        blocks.append(lax.ppermute(product, "dp", backward))
    stacked = jnp.stack(blocks)
    order = (jnp.arange(groups) - here) % groups
    mine = stacked[order].transpose(1, 0, 2).reshape(tokens_here, D)
    other_sum = swap_pair(mine)

    owners = lax.axis_size("dp") * lax.axis_size("expert")
    onehot = (expert_ids[:, :, None] == jnp.arange(owners)[None, None, :]).astype(jnp.int32)
    per_token = jnp.sum(onehot, axis=1)
    before = jnp.cumsum(per_token, axis=0) - per_token
    slot = jnp.sum(onehot * before[:, None, :], axis=-1)
    code = expert_ids * CAP + slot
    pick = (code[:, :, None] == jnp.arange(owners * CAP)[None, None, :]).astype(jnp.bfloat16)
    lanes = 128
    width = half // lanes
    lane_id = lane.astype(jnp.int32).reshape(1)
    hidden_half, outgoing = norm_dispatch(
        lane_id, mine, other_sum, residual, norm_gain.reshape(1, -1), code.T, owners * CAP
    )
    received = lax.all_to_all(
        outgoing.reshape(owners, CAP * width, lanes), ("dp", "expert"), split_axis=0, concat_axis=0, tiled=True
    ).reshape(owners * CAP * width, lanes)
    other = swap_pair(received)
    down_other = swap_pair(lax.dynamic_slice_in_dim(w_down[0], (1 - lane) * half, half, 1))
    act = gate_up(lane_id, received, other, w_gate[0], w_up[0])
    expert_out = down(lane_id, act, swap_pair(act), w_down[0], down_other)

    returned = lax.all_to_all(
        expert_out.reshape(owners, CAP * width, lanes), ("dp", "expert"), split_axis=0, concat_axis=0, tiled=True
    ).reshape(owners * CAP, width, lanes)
    picked = jnp.einsum("tkr,rjl->tkjl", pick, returned, preferred_element_type=jnp.float32)
    moe = jnp.sum(gates[:, :, None, None] * picked, axis=1).reshape(tokens_here, half)
    return (hidden_half + moe).astype(jnp.bfloat16)


def solution(mesh):
    return jax.shard_map(
        per_device,
        mesh=mesh,
        in_specs=(
            P(("dp", "expert"), "tensor"),
            P(("dp", "expert"), "tensor"),
            P(("dp", "expert"), "tensor"),
            P(("dp", "expert"), None, "tensor"),
            P(("dp", "expert"), None, "tensor"),
            P("tensor", "dp"),
            P(("dp", "expert"), None),
            P(),
            P(("dp", "expert"), None),
            P(("dp", "expert"), None),
            P(("dp", "expert"), None, "tensor"),
            P(("dp", "expert"), None, "tensor"),
            P(("dp", "expert"), "tensor", None),
        ),
        out_specs=P(("dp", "expert"), "tensor"),
        check_vma=False,
    )
```

```python
import jax
import jax.numpy as jnp
from jax import lax
from jax.experimental import pallas as pl
from jax.experimental.pallas import tpu as pltpu
from jax.sharding import PartitionSpec as P

D = 2048
HEAD_WIDTH = 128
CAP = 6


def attend_local(queries, fresh_keys, fresh_values, resident_keys, resident_values):
    tokens_here = queries.shape[0]
    kv_here = fresh_keys.shape[1] // HEAD_WIDTH
    query_group = queries.shape[1] // HEAD_WIDTH // kv_here
    context = resident_keys.shape[1]
    query_rows = queries.reshape(tokens_here, kv_here, query_group, HEAD_WIDTH)
    joined_keys = jnp.concatenate([resident_keys[0], fresh_keys], 0).reshape(
        context + tokens_here, kv_here, HEAD_WIDTH
    )
    joined_values = jnp.concatenate([resident_values[0], fresh_values], 0).reshape(
        context + tokens_here, kv_here, HEAD_WIDTH
    )
    score = jnp.einsum(
        "tjgd,sjd->jgts", query_rows, joined_keys, preferred_element_type=jnp.float32
    ) * HEAD_WIDTH ** (-0.5)
    places = jnp.arange(context + tokens_here)
    rows = jnp.arange(tokens_here)
    allowed = (places[None, :] < context) | (places[None, :] - context <= rows[:, None])
    score = jnp.where(allowed, score, jnp.float32(-1e30))
    top_score = jnp.max(score, axis=-1, keepdims=True)
    weight = jnp.exp(score - top_score)
    probs = (weight / jnp.sum(weight, axis=-1, keepdims=True)).astype(jnp.bfloat16)
    attended = jnp.einsum(
        "jgts,sjd->tjgd", probs, joined_values, preferred_element_type=jnp.float32
    )
    return attended.reshape(tokens_here, -1).astype(jnp.bfloat16)


def attention_kernel(q_ref, kn_ref, vn_ref, kr_ref, vr_ref, o_ref):
    tokens = q_ref.shape[0]
    group = q_ref.shape[1] // HEAD_WIDTH
    k_res = kr_ref[0]
    v_res = vr_ref[0]
    k_new = kn_ref[...]
    v_new = vn_ref[...]
    q = jnp.concatenate(
        [q_ref[:, g * HEAD_WIDTH:(g + 1) * HEAD_WIDTH] for g in range(group)], axis=0
    )
    rows = lax.broadcasted_iota(jnp.int32, (group * tokens, tokens), 0) % tokens
    cols = lax.broadcasted_iota(jnp.int32, (group * tokens, tokens), 1)
    visible = cols <= rows
    scale = HEAD_WIDTH ** (-0.5)
    dims = (((1,), (1,)), ((), ()))
    s_res = lax.dot_general(q, k_res, dims, preferred_element_type=jnp.float32) * scale
    s_new = lax.dot_general(q, k_new, dims, preferred_element_type=jnp.float32) * scale
    s_new = jnp.where(visible, s_new, jnp.float32(-1e30))
    top = jnp.maximum(
        jnp.max(s_res, axis=1, keepdims=True), jnp.max(s_new, axis=1, keepdims=True)
    )
    w_res = jnp.exp(s_res - top)
    w_new = jnp.exp(s_new - top)
    total = jnp.sum(w_res, axis=1, keepdims=True) + jnp.sum(w_new, axis=1, keepdims=True)
    p_res = (w_res / total).astype(jnp.bfloat16)
    p_new = (w_new / total).astype(jnp.bfloat16)
    out = jnp.dot(p_res, v_res, preferred_element_type=jnp.float32) + jnp.dot(
        p_new, v_new, preferred_element_type=jnp.float32
    )
    out = out.astype(o_ref.dtype)
    for g in range(group):
        o_ref[:, g * HEAD_WIDTH:(g + 1) * HEAD_WIDTH] = out[g * tokens:(g + 1) * tokens]


def attend_kernel(queries, fresh_keys, fresh_values, resident_keys, resident_values, interpret=False):
    tokens = queries.shape[0]
    kv_here = fresh_keys.shape[1] // HEAD_WIDTH
    width = queries.shape[1] // kv_here
    context = resident_keys.shape[1]
    return pl.pallas_call(
        attention_kernel,
        grid=(kv_here,),
        in_specs=[
            pl.BlockSpec((tokens, width), lambda j: (0, j)),
            pl.BlockSpec((tokens, HEAD_WIDTH), lambda j: (0, j)),
            pl.BlockSpec((tokens, HEAD_WIDTH), lambda j: (0, j)),
            pl.BlockSpec((1, context, HEAD_WIDTH), lambda j: (0, 0, j)),
            pl.BlockSpec((1, context, HEAD_WIDTH), lambda j: (0, 0, j)),
        ],
        out_specs=pl.BlockSpec((tokens, width), lambda j: (0, j)),
        out_shape=jax.ShapeDtypeStruct(queries.shape, jnp.bfloat16),
        interpret=interpret,
    )(queries, fresh_keys, fresh_values, resident_keys, resident_values)


def gate_up_kernel(lane_ref, mine_ref, other_ref, g_own, g_other, u_own, u_other, act_ref):
    fold = g_own.shape[0] // HEAD_WIDTH
    rows = act_ref.shape[0]
    x_mine = jnp.concatenate(
        [mine_ref[pl.ds(j, rows, stride=fold), :] for j in range(fold)], axis=1
    )
    x_other = jnp.concatenate(
        [other_ref[pl.ds(j, rows, stride=fold), :] for j in range(fold)], axis=1
    )
    gate = jnp.dot(x_mine, g_own[...], preferred_element_type=jnp.float32) + jnp.dot(
        x_other, g_other[...], preferred_element_type=jnp.float32
    )
    up = jnp.dot(x_mine, u_own[...], preferred_element_type=jnp.float32) + jnp.dot(
        x_other, u_other[...], preferred_element_type=jnp.float32
    )
    act_ref[...] = (gate / (1.0 + jnp.exp(-gate)) * up).astype(act_ref.dtype)


def down_kernel(lane_ref, act_mine, act_other, d_own, d_other, out_ref, fold_ref):
    fold = d_own.shape[1] // HEAD_WIDTH
    rows = act_mine.shape[0]
    out = jnp.dot(act_mine[...], d_own[...], preferred_element_type=jnp.float32) + jnp.dot(
        act_other[...], d_other[...], preferred_element_type=jnp.float32
    )
    for j in range(fold):
        fold_ref[pl.ds(j, rows, stride=fold), :] = out[:, j * HEAD_WIDTH:(j + 1) * HEAD_WIDTH]
    out_ref[...] = fold_ref[...].astype(out_ref.dtype)


def gate_up(lane, mine, other, gate_mat, up_mat, block_rows=256, interpret=False):
    folded, lanes = mine.shape
    half, hidden = gate_mat.shape[0] // 2, gate_mat.shape[1]
    fold = half // lanes
    rows = folded // fold
    act_spec = pl.BlockSpec((block_rows * fold, lanes), lambda i, lane_ref: (i, 0))
    own_rows = pl.BlockSpec((half, hidden), lambda i, lane_ref: (lane_ref[0], 0))
    other_rows = pl.BlockSpec((half, hidden), lambda i, lane_ref: (1 - lane_ref[0], 0))
    return pl.pallas_call(
        gate_up_kernel,
        grid_spec=pltpu.PrefetchScalarGridSpec(
            num_scalar_prefetch=1,
            grid=(rows // block_rows,),
            in_specs=[act_spec, act_spec, own_rows, other_rows, own_rows, other_rows],
            out_specs=pl.BlockSpec((block_rows, hidden), lambda i, lane_ref: (i, 0)),
        ),
        out_shape=jax.ShapeDtypeStruct((rows, hidden), jnp.bfloat16),
        interpret=interpret,
    )(lane, mine, other, gate_mat, gate_mat, up_mat, up_mat)


def down(lane, act_mine, act_other, down_mat, down_other, block_rows=256, interpret=False):
    rows, hidden = act_mine.shape
    half = down_other.shape[1]
    fold = half // HEAD_WIDTH
    act_spec = pl.BlockSpec((block_rows, hidden), lambda i, lane_ref: (i, 0))
    return pl.pallas_call(
        down_kernel,
        grid_spec=pltpu.PrefetchScalarGridSpec(
            num_scalar_prefetch=1,
            grid=(rows // block_rows,),
            in_specs=[
                act_spec,
                act_spec,
                pl.BlockSpec((hidden, half), lambda i, lane_ref: (0, lane_ref[0])),
                pl.BlockSpec((hidden, half), lambda i, lane_ref: (0, 0)),
            ],
            out_specs=pl.BlockSpec((block_rows * fold, HEAD_WIDTH), lambda i, lane_ref: (i, 0)),
            scratch_shapes=[pltpu.VMEM((block_rows * fold, HEAD_WIDTH), jnp.float32)],
        ),
        out_shape=jax.ShapeDtypeStruct((rows * fold, HEAD_WIDTH), jnp.bfloat16),
        interpret=interpret,
    )(lane, act_mine, act_other, down_mat, down_other)


def swap_pair(x):
    return lax.ppermute(x, "tensor", [(0, 1), (1, 0)])


def per_device(
    queries,
    fresh_keys,
    fresh_values,
    resident_keys,
    resident_values,
    out_weight,
    residual,
    norm_gain,
    expert_ids,
    gates,
    w_gate,
    w_up,
    w_down,
):
    tokens_here = residual.shape[0]
    lane = lax.axis_index("tensor")
    half = D // lax.axis_size("tensor")
    groups = lax.axis_size("dp")
    attended = attend_kernel(queries, fresh_keys, fresh_values, resident_keys, resident_values)

    here = lax.axis_index("dp")
    blocks = [jnp.dot(attended, out_weight, preferred_element_type=jnp.float32)]
    for shift in range(1, groups):
        onward = [(i, (i + shift) % groups) for i in range(groups)]
        backward = [(i, (i - shift) % groups) for i in range(groups)]
        arrived = lax.ppermute(attended, "dp", onward)
        product = jnp.dot(arrived, out_weight, preferred_element_type=jnp.float32)
        blocks.append(lax.ppermute(product.astype(jnp.bfloat16), "dp", backward).astype(jnp.float32))
    stacked = jnp.stack(blocks)
    order = (jnp.arange(groups) - here) % groups
    mine = stacked[order].transpose(1, 0, 2).reshape(tokens_here, D)
    summed = mine + swap_pair(mine)
    hidden = residual.astype(jnp.float32) + summed
    mean_square = jnp.mean(hidden * hidden, axis=-1, keepdims=True)
    normed = (hidden * lax.rsqrt(mean_square + 1e-06) * norm_gain).astype(jnp.bfloat16)
    hidden_half = lax.dynamic_slice_in_dim(hidden, lane * half, half, 1)
    normed_half = lax.dynamic_slice_in_dim(normed, lane * half, half, 1)

    owners = lax.axis_size("dp") * lax.axis_size("expert")
    onehot = (expert_ids[:, :, None] == jnp.arange(owners)[None, None, :]).astype(jnp.int32)
    per_token = jnp.sum(onehot, axis=1)
    before = jnp.cumsum(per_token, axis=0) - per_token
    slot = jnp.sum(onehot * before[:, None, :], axis=-1)
    code = expert_ids * CAP + slot
    pick = (code[:, :, None] == jnp.arange(owners * CAP)[None, None, :]).astype(jnp.bfloat16)
    spread = jnp.sum(pick, axis=1)
    lanes = 128
    width = half // lanes
    outgoing = jnp.einsum(
        "tr,tjl->rjl", spread, normed_half.reshape(tokens_here, width, lanes),
        preferred_element_type=jnp.float32,
    ).astype(jnp.bfloat16)
    received = lax.all_to_all(
        outgoing.reshape(owners, CAP * width, lanes), ("dp", "expert"), split_axis=0, concat_axis=0, tiled=True
    ).reshape(owners * CAP * width, lanes)
    other = swap_pair(received)
    lane_id = lane.astype(jnp.int32).reshape(1)
    down_other = swap_pair(lax.dynamic_slice_in_dim(w_down[0], (1 - lane) * half, half, 1))
    act = gate_up(lane_id, received, other, w_gate[0], w_up[0])
    expert_out = down(lane_id, act, swap_pair(act), w_down[0], down_other)

    returned = lax.all_to_all(
        expert_out.reshape(owners, CAP * width, lanes), ("dp", "expert"), split_axis=0, concat_axis=0, tiled=True
    ).reshape(owners * CAP, width, lanes)
    picked = jnp.einsum("tkr,rjl->tkjl", pick, returned, preferred_element_type=jnp.float32)
    moe = jnp.sum(gates[:, :, None, None] * picked, axis=1).reshape(tokens_here, half)
    return (hidden_half + moe).astype(jnp.bfloat16)


def solution(mesh):
    return jax.shard_map(
        per_device,
        mesh=mesh,
        in_specs=(
            P(("dp", "expert"), "tensor"),
            P(("dp", "expert"), "tensor"),
            P(("dp", "expert"), "tensor"),
            P(("dp", "expert"), None, "tensor"),
            P(("dp", "expert"), None, "tensor"),
            P("tensor", "dp"),
            P(("dp", "expert"), None),
            P(),
            P(("dp", "expert"), None),
            P(("dp", "expert"), None),
            P(("dp", "expert"), None, "tensor"),
            P(("dp", "expert"), None, "tensor"),
            P(("dp", "expert"), "tensor", None),
        ),
        out_specs=P(("dp", "expert"), "tensor"),
        check_vma=False,
    )
```

```python
import jax
import jax.numpy as jnp
from jax import lax
from jax.experimental import pallas as pl
from jax.experimental.pallas import tpu as pltpu
from jax.sharding import PartitionSpec as P

D = 2048
HEAD_WIDTH = 128
CAP = 6


def attend_local(queries, fresh_keys, fresh_values, resident_keys, resident_values):
    tokens_here = queries.shape[0]
    kv_here = fresh_keys.shape[1] // HEAD_WIDTH
    query_group = queries.shape[1] // HEAD_WIDTH // kv_here
    context = resident_keys.shape[1]
    query_rows = queries.reshape(tokens_here, kv_here, query_group, HEAD_WIDTH)
    joined_keys = jnp.concatenate([resident_keys[0], fresh_keys], 0).reshape(
        context + tokens_here, kv_here, HEAD_WIDTH
    )
    joined_values = jnp.concatenate([resident_values[0], fresh_values], 0).reshape(
        context + tokens_here, kv_here, HEAD_WIDTH
    )
    score = jnp.einsum(
        "tjgd,sjd->jgts", query_rows, joined_keys, preferred_element_type=jnp.float32
    ) * HEAD_WIDTH ** (-0.5)
    places = jnp.arange(context + tokens_here)
    rows = jnp.arange(tokens_here)
    allowed = (places[None, :] < context) | (places[None, :] - context <= rows[:, None])
    score = jnp.where(allowed, score, jnp.float32(-1e30))
    top_score = jnp.max(score, axis=-1, keepdims=True)
    weight = jnp.exp(score - top_score)
    probs = (weight / jnp.sum(weight, axis=-1, keepdims=True)).astype(jnp.bfloat16)
    attended = jnp.einsum(
        "jgts,sjd->tjgd", probs, joined_values, preferred_element_type=jnp.float32
    )
    return attended.reshape(tokens_here, -1).astype(jnp.bfloat16)


def attention_kernel(q_ref, kn_ref, vn_ref, kr_ref, vr_ref, o_ref):
    tokens = q_ref.shape[0]
    group = q_ref.shape[1] // HEAD_WIDTH
    k_res = kr_ref[0]
    v_res = vr_ref[0]
    k_new = kn_ref[...]
    v_new = vn_ref[...]
    q = jnp.concatenate(
        [q_ref[:, g * HEAD_WIDTH:(g + 1) * HEAD_WIDTH] for g in range(group)], axis=0
    )
    rows = lax.broadcasted_iota(jnp.int32, (group * tokens, tokens), 0) % tokens
    cols = lax.broadcasted_iota(jnp.int32, (group * tokens, tokens), 1)
    visible = cols <= rows
    scale = HEAD_WIDTH ** (-0.5)
    dims = (((1,), (1,)), ((), ()))
    s_res = lax.dot_general(q, k_res, dims, preferred_element_type=jnp.float32) * scale
    s_new = lax.dot_general(q, k_new, dims, preferred_element_type=jnp.float32) * scale
    s_new = jnp.where(visible, s_new, jnp.float32(-1e30))
    top = jnp.maximum(
        jnp.max(s_res, axis=1, keepdims=True), jnp.max(s_new, axis=1, keepdims=True)
    )
    w_res = jnp.exp(s_res - top)
    w_new = jnp.exp(s_new - top)
    total = jnp.sum(w_res, axis=1, keepdims=True) + jnp.sum(w_new, axis=1, keepdims=True)
    p_res = (w_res / total).astype(jnp.bfloat16)
    p_new = (w_new / total).astype(jnp.bfloat16)
    out = jnp.dot(p_res, v_res, preferred_element_type=jnp.float32) + jnp.dot(
        p_new, v_new, preferred_element_type=jnp.float32
    )
    out = out.astype(o_ref.dtype)
    for g in range(group):
        o_ref[:, g * HEAD_WIDTH:(g + 1) * HEAD_WIDTH] = out[g * tokens:(g + 1) * tokens]


def attend_kernel(queries, fresh_keys, fresh_values, resident_keys, resident_values, interpret=False):
    tokens = queries.shape[0]
    kv_here = fresh_keys.shape[1] // HEAD_WIDTH
    width = queries.shape[1] // kv_here
    context = resident_keys.shape[1]
    return pl.pallas_call(
        attention_kernel,
        grid=(kv_here,),
        in_specs=[
            pl.BlockSpec((tokens, width), lambda j: (0, j)),
            pl.BlockSpec((tokens, HEAD_WIDTH), lambda j: (0, j)),
            pl.BlockSpec((tokens, HEAD_WIDTH), lambda j: (0, j)),
            pl.BlockSpec((1, context, HEAD_WIDTH), lambda j: (0, 0, j)),
            pl.BlockSpec((1, context, HEAD_WIDTH), lambda j: (0, 0, j)),
        ],
        out_specs=pl.BlockSpec((tokens, width), lambda j: (0, j)),
        out_shape=jax.ShapeDtypeStruct(queries.shape, jnp.bfloat16),
        interpret=interpret,
    )(queries, fresh_keys, fresh_values, resident_keys, resident_values)


def gate_up_kernel(lane_ref, mine_ref, other_ref, g_own, g_other, u_own, u_other, act_ref):
    fold = g_own.shape[0] // HEAD_WIDTH
    rows = act_ref.shape[0]
    x_mine = jnp.concatenate(
        [mine_ref[pl.ds(j, rows, stride=fold), :] for j in range(fold)], axis=1
    )
    x_other = jnp.concatenate(
        [other_ref[pl.ds(j, rows, stride=fold), :] for j in range(fold)], axis=1
    )
    gate = jnp.dot(x_mine, g_own[...], preferred_element_type=jnp.float32) + jnp.dot(
        x_other, g_other[...], preferred_element_type=jnp.float32
    )
    up = jnp.dot(x_mine, u_own[...], preferred_element_type=jnp.float32) + jnp.dot(
        x_other, u_other[...], preferred_element_type=jnp.float32
    )
    act_ref[...] = (gate / (1.0 + jnp.exp(-gate)) * up).astype(act_ref.dtype)


def down_kernel(lane_ref, act_mine, act_other, d_own, d_other, out_ref, fold_ref):
    fold = d_own.shape[1] // HEAD_WIDTH
    rows = act_mine.shape[0]
    out = jnp.dot(act_mine[...], d_own[...], preferred_element_type=jnp.float32) + jnp.dot(
        act_other[...], d_other[...], preferred_element_type=jnp.float32
    )
    for j in range(fold):
        fold_ref[pl.ds(j, rows, stride=fold), :] = out[:, j * HEAD_WIDTH:(j + 1) * HEAD_WIDTH]
    out_ref[...] = fold_ref[...].astype(out_ref.dtype)


def gate_up(lane, mine, other, gate_mat, up_mat, block_rows=256, interpret=False):
    folded, lanes = mine.shape
    half, hidden = gate_mat.shape[0] // 2, gate_mat.shape[1]
    fold = half // lanes
    rows = folded // fold
    act_spec = pl.BlockSpec((block_rows * fold, lanes), lambda i, lane_ref: (i, 0))
    own_rows = pl.BlockSpec((half, hidden), lambda i, lane_ref: (lane_ref[0], 0))
    other_rows = pl.BlockSpec((half, hidden), lambda i, lane_ref: (1 - lane_ref[0], 0))
    return pl.pallas_call(
        gate_up_kernel,
        grid_spec=pltpu.PrefetchScalarGridSpec(
            num_scalar_prefetch=1,
            grid=(rows // block_rows,),
            in_specs=[act_spec, act_spec, own_rows, other_rows, own_rows, other_rows],
            out_specs=pl.BlockSpec((block_rows, hidden), lambda i, lane_ref: (i, 0)),
        ),
        out_shape=jax.ShapeDtypeStruct((rows, hidden), jnp.bfloat16),
        interpret=interpret,
    )(lane, mine, other, gate_mat, gate_mat, up_mat, up_mat)


def down(lane, act_mine, act_other, down_mat, down_other, block_rows=768, interpret=False):
    rows, hidden = act_mine.shape
    half = down_other.shape[1]
    fold = half // HEAD_WIDTH
    act_spec = pl.BlockSpec((block_rows, hidden), lambda i, lane_ref: (i, 0))
    return pl.pallas_call(
        down_kernel,
        grid_spec=pltpu.PrefetchScalarGridSpec(
            num_scalar_prefetch=1,
            grid=(rows // block_rows,),
            in_specs=[
                act_spec,
                act_spec,
                pl.BlockSpec((hidden, half), lambda i, lane_ref: (0, lane_ref[0])),
                pl.BlockSpec((hidden, half), lambda i, lane_ref: (0, 0)),
            ],
            out_specs=pl.BlockSpec((block_rows * fold, HEAD_WIDTH), lambda i, lane_ref: (i, 0)),
            scratch_shapes=[pltpu.VMEM((block_rows * fold, HEAD_WIDTH), jnp.float32)],
        ),
        out_shape=jax.ShapeDtypeStruct((rows * fold, HEAD_WIDTH), jnp.bfloat16),
        interpret=interpret,
    )(lane, act_mine, act_other, down_mat, down_other)


def swap_pair(x):
    return lax.ppermute(x, "tensor", [(0, 1), (1, 0)])


def per_device(
    queries,
    fresh_keys,
    fresh_values,
    resident_keys,
    resident_values,
    out_weight,
    residual,
    norm_gain,
    expert_ids,
    gates,
    w_gate,
    w_up,
    w_down,
):
    tokens_here = residual.shape[0]
    lane = lax.axis_index("tensor")
    half = D // lax.axis_size("tensor")
    groups = lax.axis_size("dp")
    attended = attend_kernel(queries, fresh_keys, fresh_values, resident_keys, resident_values)

    here = lax.axis_index("dp")
    blocks = [jnp.dot(attended, out_weight, preferred_element_type=jnp.float32)]
    for shift in range(1, groups):
        onward = [(i, (i + shift) % groups) for i in range(groups)]
        backward = [(i, (i - shift) % groups) for i in range(groups)]
        arrived = lax.ppermute(attended, "dp", onward)
        product = jnp.dot(arrived, out_weight, preferred_element_type=jnp.float32)
        blocks.append(lax.ppermute(product, "dp", backward))
    stacked = jnp.stack(blocks)
    order = (jnp.arange(groups) - here) % groups
    mine = stacked[order].transpose(1, 0, 2).reshape(tokens_here, D)
    summed = mine + swap_pair(mine)
    hidden = residual.astype(jnp.float32) + summed
    mean_square = jnp.mean(hidden * hidden, axis=-1, keepdims=True)
    normed = (hidden * lax.rsqrt(mean_square + 1e-06) * norm_gain).astype(jnp.bfloat16)
    hidden_half = lax.dynamic_slice_in_dim(hidden, lane * half, half, 1)
    normed_half = lax.dynamic_slice_in_dim(normed, lane * half, half, 1)

    owners = lax.axis_size("dp") * lax.axis_size("expert")
    onehot = (expert_ids[:, :, None] == jnp.arange(owners)[None, None, :]).astype(jnp.int32)
    per_token = jnp.sum(onehot, axis=1)
    before = jnp.cumsum(per_token, axis=0) - per_token
    slot = jnp.sum(onehot * before[:, None, :], axis=-1)
    code = expert_ids * CAP + slot
    pick = (code[:, :, None] == jnp.arange(owners * CAP)[None, None, :]).astype(jnp.bfloat16)
    spread = jnp.sum(pick, axis=1)
    lanes = 128
    width = half // lanes
    outgoing = jnp.einsum(
        "tr,tjl->rjl", spread, normed_half.reshape(tokens_here, width, lanes),
        preferred_element_type=jnp.float32,
    ).astype(jnp.bfloat16)
    received = lax.all_to_all(
        outgoing.reshape(owners, CAP * width, lanes), ("dp", "expert"), split_axis=0, concat_axis=0, tiled=True
    ).reshape(owners * CAP * width, lanes)
    other = swap_pair(received)
    lane_id = lane.astype(jnp.int32).reshape(1)
    down_other = swap_pair(lax.dynamic_slice_in_dim(w_down[0], (1 - lane) * half, half, 1))
    act = gate_up(lane_id, received, other, w_gate[0], w_up[0])
    expert_out = down(lane_id, act, swap_pair(act), w_down[0], down_other)

    returned = lax.all_to_all(
        expert_out.reshape(owners, CAP * width, lanes), ("dp", "expert"), split_axis=0, concat_axis=0, tiled=True
    ).reshape(owners * CAP, width, lanes)
    picked = jnp.einsum("tkr,rjl->tkjl", pick, returned, preferred_element_type=jnp.float32)
    moe = jnp.sum(gates[:, :, None, None] * picked, axis=1).reshape(tokens_here, half)
    return (hidden_half + moe).astype(jnp.bfloat16)


def solution(mesh):
    return jax.shard_map(
        per_device,
        mesh=mesh,
        in_specs=(
            P(("dp", "expert"), "tensor"),
            P(("dp", "expert"), "tensor"),
            P(("dp", "expert"), "tensor"),
            P(("dp", "expert"), None, "tensor"),
            P(("dp", "expert"), None, "tensor"),
            P("tensor", "dp"),
            P(("dp", "expert"), None),
            P(),
            P(("dp", "expert"), None),
            P(("dp", "expert"), None),
            P(("dp", "expert"), None, "tensor"),
            P(("dp", "expert"), None, "tensor"),
            P(("dp", "expert"), "tensor", None),
        ),
        out_specs=P(("dp", "expert"), "tensor"),
        check_vma=False,
    )
```
